32 devices in a mesh: gx: 4 (over x, core), gy: 4 (over z), gz: 2 (over y).
Axes of the slice: x: 2, y: 2, z: 4, core: 2. Of those that a mesh axis runs over, the one named last changes fastest.
Arguments:
- wave: float32 [64, 128, 256], P('gx', 'gy', 'gz'), may hold values from -7 to 7
- external: float32 [64, 128, 256], P('gx', 'gy', 'gz'), may hold values from 0 to 2
- weights: float32 [3, 17], replicated, may hold values from 0.02 to 0.1
Outputs:
- wave_next: float32 [64, 128, 256], P('gx', 'gy', 'gz')
- correlation: float32 [64, 128, 256], P('gx', 'gy', 'gz')
The draws below stay inside these ranges and needn't reach their ends.
All inputs are finite; a program needn't handle non-finite values.
Results may differ from the reference program's by a relative error of at most 0.00029.
Values sent between devices are 32-bit elements; how exact they have to be, the bound alone decides.
A program may use at most 64 MiB of HBM per device.

```python
import math
import jax
import jax.numpy as jnp
from jax import lax

CX = 16
CY = 32
CZ = 128
SUBSTEPS = 3
NX = 64
NY = 128
NZ = 256


def tile_levels(key, low, high):
    level_key, shift_key = jax.random.split(key)
    counts = (NX // CX, NY // CY, NZ // CZ)
    logs = jax.random.uniform(level_key, counts, jnp.float32, jnp.log(low), jnp.log(high))
    levels = jnp.exp(logs)
    levels = jnp.repeat(levels, CX, axis=0)
    levels = jnp.repeat(levels, CY, axis=1)
    levels = jnp.repeat(levels, CZ, axis=2)
    shifts = jax.random.randint(shift_key, (3,), 0, 4)
    levels = jnp.roll(levels, shifts[0], axis=0)
    levels = jnp.roll(levels, shifts[1], axis=1)
    levels = jnp.roll(levels, shifts[2], axis=2)
    return levels


def draw_wave(key, part):
    first = jax.random.fold_in(key, 0)
    rise = 1.0 + 0.732 * jnp.arange(NX, dtype=jnp.float32) / max(NX - 1, 1)
    amplitude = tile_levels(jax.random.fold_in(key, 11), 0.45, 1.1)
    rough = jnp.clip(jax.random.normal(first, (NX, NY, NZ), jnp.float32), -4.0, 4.0)
    values = rough * rise[:, None, None] * amplitude
    return jnp.clip(values, -7.0, 7.0).astype(jnp.float32)


def draw_external(key, part):
    first, second = jax.random.split(jax.random.fold_in(key, 23))
    levels = tile_levels(first, 0.15, 1.0)
    rough = jnp.exp(jax.random.uniform(second, (NX, NY, NZ), jnp.float32, jnp.log(0.5), jnp.log(2.0)))
    return jnp.clip(levels * rough, 0.0, 2.0).astype(jnp.float32)


def setup_inputs(seed: int = 0) -> dict:
    key_of = jax.random.split(jax.random.key(seed), 4)
    return {
        "wave": draw_wave(jax.random.fold_in(key_of[3], 71), 0),
        "external": draw_external(jax.random.fold_in(key_of[3], 71), 0),
        "weights": jnp.clip(jnp.exp(jax.random.uniform(key_of[2], (3, 17), jnp.float32, math.log(0.02), math.log(0.1))), 0.02, 0.1),
    }


LAP_COEF = (-205.0 / 72.0, 8.0 / 5.0, -1.0 / 5.0, 8.0 / 315.0, -1.0 / 560.0)

def smear(field, weights, flip):
    for dim in range(3):
        length = field.shape[dim]
        widths = [(0, 0), (0, 0), (0, 0)]
        widths[dim] = (8, 8)
        padded = jnp.pad(field, widths)
        total = jnp.zeros_like(field)
        for tap in range(17):
            coef = weights[dim, 16 - tap] if flip else weights[dim, tap]
            total = total + coef * lax.slice_in_dim(padded, tap, tap + length, axis=dim)
        field = total
    return field

def laplace(field):
    padded = jnp.pad(field, 4)
    total = 3.0 * LAP_COEF[0] * field
    for dim in range(3):
        length = field.shape[dim]
        inner = [slice(4, -4), slice(4, -4), slice(4, -4)]
        for step in range(1, 5):
            upper = list(inner)
            lower = list(inner)
            upper[dim] = slice(4 + step, 4 + step + length)
            lower[dim] = slice(4 - step, 4 - step + length)
            total = total + LAP_COEF[step] * (padded[tuple(upper)] + padded[tuple(lower)])
    return total

def reference(wave, external, weights):
    density = wave * wave
    coarse = smear(density, weights, False)
    source = -1.0 * density * coarse + 0.5 * density * coarse * coarse
    correlation = -0.5 * coarse * coarse + 0.5 / 3.0 * coarse * coarse * coarse + smear(source, weights, True)
    potential = correlation + external
    psi = wave
    for step in range(SUBSTEPS):
        psi = psi - 0.08 * (-0.5 * laplace(psi) + potential * psi)
    total = jnp.sum(psi * psi)
    wave_next = psi * lax.rsqrt(total / (NX * NY * NZ) + 1e-06)
    return (wave_next, correlation)
```

```python
import functools

import jax
import jax.numpy as jnp
from jax import lax
from jax.experimental import pallas as pl
from jax.experimental.pallas import tpu as pltpu
from jax.sharding import PartitionSpec as P

SUBSTEPS = 3
LAP_COEF = (-205.0 / 72.0, 8.0 / 5.0, -1.0 / 5.0, 8.0 / 315.0, -1.0 / 560.0)
STEP = 0.08
AXES = ("gx", "gy", "gz")
MESH = pl.DeviceIdType.MESH
R = 8
H = 4


def lanes(shape):
    return lax.broadcasted_iota(jnp.int32, shape, len(shape) - 1)


def lane_taps(mid, low, high, step, taps):
    at = lanes(mid.shape)
    width = mid.shape[-1]
    total = None
    for k, tap in taps:
        if k == 0:
            part = mid
        elif k > 0:
            s = k * step
            part = pltpu.roll(jnp.where(at < s, high, mid), width - s, mid.ndim - 1)
        else:
            s = -k * step
            part = pltpu.roll(jnp.where(at >= width - s, low, mid), s, mid.ndim - 1)
        part = part * tap
        total = part if total is None else total + part
    return total


def kernel(sizes, w_ref, wave_ref, ext_ref, out_ref, corr_ref,
           wb, sb, xc, yb, pyb, psi, va, pack, zin, sums, sums2,
           send, recv, send2, recv2):
    nx, ny, nz = sizes
    cx, cy, cz = wave_ref.shape
    ix, iy, iz = (lax.axis_index(a) for a in AXES)
    plane = nx * nz
    per = cz // cx
    here = ix * nz + iz

    def plane_id(d):
        t = lax.rem(here + d, plane)
        return t, {"gx": lax.div(t, nz), "gz": lax.rem(t, nz)}

    def line_id(d):
        t = lax.rem(iy + d, ny)
        return t, {"gy": t}

    barrier = pltpu.get_barrier_semaphore()

    def greet(ids):
        def body(d, c):
            pl.semaphore_signal(barrier, inc=1, device_id=ids(d)[1], device_id_type=MESH)
            return c
        return body

    lax.fori_loop(1, plane, greet(plane_id), 0)
    lax.fori_loop(1, ny, greet(line_id), 0)

    counter = [0]

    def message(src, dst, dx, dy, dz):
        k = counter[0]
        counter[0] += 1
        to, back = None, None
        for d, i, n in ((dx, ix, nx), (dy, iy, ny), (dz, iz, nz)):
            if d > 0:
                a, b = i < n - 1, i > 0
            elif d < 0:
                a, b = i > 0, i < n - 1
            else:
                continue
            to = a if to is None else to & a
            back = b if back is None else back & b
        target = {}
        for name, d, i, n in zip(AXES, (dx, dy, dz), (ix, iy, iz), sizes):
            if d:
                target[name] = jnp.clip(i + d, 0, n - 1)
        copy = pltpu.make_async_remote_copy(
            src_ref=src, dst_ref=dst, send_sem=send.at[k], recv_sem=recv.at[k],
            device_id=target, device_id_type=MESH)
        return copy, to, back, dst

    sent = []

    def start(messages):
        for copy, to, _, _ in messages:
            pl.when(to)(copy.start)
            sent.append((copy, to))

    def blank(messages):
        for _, _, back, dst in messages:
            @pl.when(jnp.logical_not(back))
            def _(dst=dst):
                dst[...] = jnp.zeros(dst.shape, dst.dtype)

    def arrive(messages):
        for copy, _, back, _ in messages:
            pl.when(back)(copy.wait_recv)

    at = lanes((cy, cz))
    zero = jnp.zeros((cy, cz), jnp.float32)

    def pack_one(i, value, packs):
        mine = (at >= per * i) & (at < per * i + per)
        low = pltpu.roll(value, per * i, 1)
        high = pltpu.roll(value, lax.rem(per * i + per, cz), 1)
        return jnp.where(mine, low, packs[0]), jnp.where(mine, high, packs[1])

    def unpack(i, from_low, from_high):
        a = pltpu.roll(from_high, lax.rem(cz - per * i, cz), 1)
        b = pltpu.roll(from_low, cz - per - per * i, 1)
        return jnp.where(at < per, a, b)

    def pack_out(slot, packs):
        pack[slot, 0] = packs[0]
        pack[slot, 1] = packs[1]

    def z_messages(slot, across):
        out = []
        for dx in ((-1, 0, 1) if across else (0,)):
            out.append(message(pack.at[slot, 1], zin.at[slot, 0, 1 - dx], dx, 0, 1))
            out.append(message(pack.at[slot, 0], zin.at[slot, 1, 1 - dx], dx, 0, -1))
        return out

    def stage(i, packs):
        value = wave_ref[i]
        wb[R + i, pl.ds(R, cy)] = value
        return pack_one(i, value, packs)

    pack_out(0, lax.fori_loop(0, cx, stage, (zero, zero)))

    wave_x = [
        message(wave_ref.at[pl.ds(cx - R, R)], wb.at[pl.ds(0, R), pl.ds(R, cy)], 1, 0, 0),
        message(wave_ref.at[pl.ds(0, R)], wb.at[pl.ds(R + cx, R), pl.ds(R, cy)], -1, 0, 0),
    ]
    wave_z = z_messages(0, True)
    wave_y = [
        message(wave_ref.at[:, pl.ds(cy - R, R)], wb.at[pl.ds(R, cx), pl.ds(0, R)], 0, 1, 0),
        message(wave_ref.at[:, pl.ds(0, R)], wb.at[pl.ds(R, cx), pl.ds(R + cy, R)], 0, -1, 0),
    ]

    def y_messages(buf):
        return [
            message(buf.at[:, pl.ds(cy, R)], buf.at[:, pl.ds(0, R)], 0, 1, 0),
            message(buf.at[:, pl.ds(R, R)], buf.at[:, pl.ds(R + cy, R)], 0, -1, 0),
        ]

    mid_y = y_messages(yb.at[0])
    src_x = [
        message(sb.at[pl.ds(cx, R)], sb.at[pl.ds(0, R)], 1, 0, 0),
        message(sb.at[pl.ds(R, R)], sb.at[pl.ds(R + cx, R)], -1, 0, 0),
    ]
    src_z = z_messages(1, True)
    end_y = y_messages(yb.at[1])

    psi_moves = []
    for s in range(SUBSTEPS - 1):
        buf = psi.at[s]
        moves = [
            message(buf.at[pl.ds(cx, H), pl.ds(R, cy)], buf.at[pl.ds(0, H), pl.ds(R, cy)], 1, 0, 0),
            message(buf.at[pl.ds(H, H), pl.ds(R, cy)], buf.at[pl.ds(H + cx, H), pl.ds(R, cy)], -1, 0, 0),
        ]
        own = pl.ds(H, cx)
        moves += [
            message(buf.at[own, pl.ds(cy, R)], buf.at[own, pl.ds(0, R)], 0, 1, 0),
            message(buf.at[own, pl.ds(R, R)], buf.at[own, pl.ds(R + cy, R)], 0, -1, 0),
        ]
        moves += z_messages(2 + s, False)
        psi_moves.append(moves)

    pl.semaphore_wait(barrier, plane - 1 + ny - 1)
    start(wave_x + wave_z + wave_y)
    for group in [wave_x, wave_z, wave_y, mid_y, src_x, src_z, end_y] + psi_moves:
        blank(group)

    def taps_of(dim, flip):
        return [(k, w_ref[dim, R - k if flip else R + k]) for k in range(-R, R + 1)]

    def smear_xz(src, y_at, slot, square, flip, buf):
        taps = taps_of(0, flip)

        def x_pass(j, c):
            rows = pl.ds(pl.multiple_of(y_at + 8 * j, 8), 8)
            ins = [src[k, rows] for k in range(cx + 2 * R)]
            if square:
                ins = [v * v for v in ins]
            for i in range(cx):
                total = None
                for k, tap in taps:
                    part = ins[i + R + k] * tap
                    total = part if total is None else total + part
                xc[i, pl.ds(pl.multiple_of(8 * j, 8), 8)] = total
            return c

        lax.fori_loop(0, cy // 8, x_pass, 0)
        sides = []
        for side in range(2):
            near = [zin[slot, side, place] for place in range(3)]
            if square:
                near = [v * v for v in near]
            sides.append(near)
        below = lane_taps(sides[0][1], sides[0][0], sides[0][2], per, taps)
        above = lane_taps(sides[1][1], sides[1][0], sides[1][2], per, taps)
        taps_z = taps_of(2, flip)

        def z_pass(i, c):
            near = unpack(i, below, above)
            buf[i, pl.ds(R, cy)] = lane_taps(xc[i], near, near, 1, taps_z)
            return c

        lax.fori_loop(0, cx, z_pass, 0)

    def smear_y(buf, i, taps):
        total = None
        for k, tap in taps:
            part = buf[i, pl.ds(R + k, cy)] * tap
            total = part if total is None else total + part
        return total

    arrive(wave_x + wave_z)
    smear_xz(wb, R, 0, True, False, yb.at[0])
    start(mid_y)
    arrive(mid_y)
    taps_y = taps_of(1, False)

    def source_pass(i, packs):
        coarse = smear_y(yb.at[0], i, taps_y)
        value = wave_ref[i]
        dens = value * value
        both = coarse * coarse
        source = 0.5 * dens * both - dens * coarse
        corr_ref[i] = (0.5 / 3.0) * both * coarse - 0.5 * both
        sb[R + i] = source
        return pack_one(i, source, packs)

    pack_out(1, lax.fori_loop(0, cx, source_pass, (zero, zero)))

    start(src_x + src_z)
    arrive(src_x + src_z)
    smear_xz(sb, 0, 1, False, True, yb.at[1])
    start(end_y)
    arrive(end_y)
    taps_yt = taps_of(1, True)

    def corr_pass(i, c):
        corr = corr_ref[i] + smear_y(yb.at[1], i, taps_yt)
        corr_ref[i] = corr
        va[i] = (1.0 + STEP * 0.5 * 3.0 * LAP_COEF[0]) - STEP * (corr + ext_ref[i])
        return c

    lax.fori_loop(0, cx, corr_pass, 0)

    gains = [STEP * 0.5 * c for c in LAP_COEF]

    def advance(buf, reach, i, below, above):
        center = buf[reach + i, pl.ds(R, cy)]
        near = unpack(i, below, above)
        total = center * va[i]
        for k in range(1, H + 1):
            pair = buf[reach + i + k, pl.ds(R, cy)] + buf[reach + i - k, pl.ds(R, cy)]
            pair += buf[reach + i, pl.ds(R + k, cy)] + buf[reach + i, pl.ds(R - k, cy)]
            pair += pltpu.roll(jnp.where(at < k, near, center), cz - k, 1)
            pair += pltpu.roll(jnp.where(at >= cz - k, near, center), k, 1)
            total += gains[k] * pair
        return total

    arrive(wave_y)
    buf, reach, slot = wb, R, 0
    for s in range(SUBSTEPS):
        if s:
            arrive(psi_moves[s - 1])
        below, above = zin[slot, 0, 1], zin[slot, 1, 1]
        if s < SUBSTEPS - 1:
            after = psi.at[s]

            def middle(i, packs, buf=buf, reach=reach, below=below, above=above, after=after):
                value = advance(buf, reach, i, below, above)
                after[H + i, pl.ds(R, cy)] = value
                return pack_one(i, value, packs)

            pack_out(2 + s, lax.fori_loop(0, cx, middle, (zero, zero)))
            start(psi_moves[s])
            buf, reach, slot = after, H, 2 + s
        else:
            def last(i, total):
                value = advance(buf, reach, i, below, above)
                out_ref[i] = value
                return total + value * value

            total = lax.fori_loop(0, cx, last, zero)

    part = total[0:8]
    for j in range(1, cy // 8):
        part = part + total[8 * j:8 * j + 8]

    def all_sum(part, slots, ssem, rsem, me, n, ids):
        if n == 1:
            return part
        slots[n] = part

        def copy_of(d, slot):
            return pltpu.make_async_remote_copy(
                src_ref=slots.at[n], dst_ref=slots.at[slot], send_sem=ssem.at[d], recv_sem=rsem.at[slot],
                device_id=ids(d)[1], device_id_type=MESH)

        def go(d, c):
            copy_of(d, me).start()
            return c

        def come(d, c):
            t = ids(d)[0]
            copy_of(d, t).wait_recv()
            return c + slots[t]

        def left(d, c):
            copy_of(d, me).wait_send()
            return c

        lax.fori_loop(1, n, go, 0)
        total = lax.fori_loop(1, n, come, part)
        lax.fori_loop(1, n, left, 0)
        return total

    part = all_sum(part, sums, send2.at[0], recv2.at[0], here, plane, plane_id)
    part = all_sum(part, sums2, send2.at[1], recv2.at[1], iy, ny, line_id)
    cells = float(cx * cy * cz * nx * ny * nz)
    scale = lax.rsqrt(jnp.full((1, cz), jnp.sum(part), jnp.float32) / cells + 1e-06)

    def finish(i, c):
        out_ref[i] = out_ref[i] * scale
        return c

    lax.fori_loop(0, cx, finish, 0)
    for copy, to in sent:
        pl.when(to)(copy.wait_send)


def shards(sizes, wave, external, weights):
    cx, cy, cz = wave.shape
    nx, ny, nz = sizes
    f32 = jnp.float32
    n_messages = 36
    most = max(nx * nz, ny)
    vmem = pl.BlockSpec(memory_space=pltpu.VMEM)
    return pl.pallas_call(
        functools.partial(kernel, sizes),
        out_shape=(jax.ShapeDtypeStruct(wave.shape, f32), jax.ShapeDtypeStruct(wave.shape, f32)),
        in_specs=[pl.BlockSpec(memory_space=pltpu.SMEM), vmem, vmem],
        out_specs=(vmem, vmem),
        scratch_shapes=[
            pltpu.VMEM((cx + 2 * R, cy + 2 * R, cz), f32),
            pltpu.VMEM((cx + 2 * R, cy, cz), f32),
            pltpu.VMEM((cx, cy, cz), f32),
            pltpu.VMEM((2, cx, cy + 2 * R, cz), f32),
            pltpu.VMEM((8, cz), f32),
            pltpu.VMEM((SUBSTEPS - 1, cx + 2 * H, cy + 2 * R, cz), f32),
            pltpu.VMEM((cx, cy, cz), f32),
            pltpu.VMEM((SUBSTEPS + 1, 2, cy, cz), f32),
            pltpu.VMEM((SUBSTEPS + 1, 2, 3, cy, cz), f32),
            pltpu.VMEM((nx * nz + 1, 8, cz), f32),
            pltpu.VMEM((ny + 1, 8, cz), f32),
            pltpu.SemaphoreType.DMA((n_messages,)),
            pltpu.SemaphoreType.DMA((n_messages,)),
            pltpu.SemaphoreType.DMA((2, most)),
            pltpu.SemaphoreType.DMA((2, most)),
        ],
        compiler_params=pltpu.CompilerParams(collective_id=0, has_side_effects=True,
                                             vmem_limit_bytes=32 * 1024 * 1024),
    )(weights, wave, external)


def solution(mesh):
    sizes = tuple(mesh.shape[a] for a in AXES)
    spec = P(*AXES)
    return jax.shard_map(
        functools.partial(shards, sizes),
        mesh=mesh,
        in_specs=(spec, spec, P()),
        out_specs=(spec, spec),
        check_vma=False,
    )
```

```python
import functools

import jax
import jax.numpy as jnp
from jax import lax
from jax.experimental import pallas as pl
from jax.experimental.pallas import tpu as pltpu
from jax.sharding import PartitionSpec as P

SUBSTEPS = 3
LAP_COEF = (-205.0 / 72.0, 8.0 / 5.0, -1.0 / 5.0, 8.0 / 315.0, -1.0 / 560.0)
STEP = 0.08
AXES = ("gx", "gy", "gz")
MESH = pl.DeviceIdType.MESH
R = 8
H = 4


def lanes(shape):
    return lax.broadcasted_iota(jnp.int32, shape, len(shape) - 1)


def lane_taps(mid, low, high, step, taps):
    at = lanes(mid.shape)
    width = mid.shape[-1]
    total = None
    for k, tap in taps:
        if k == 0:
            part = mid
        elif k > 0:
            s = k * step
            part = pltpu.roll(jnp.where(at < s, high, mid), width - s, mid.ndim - 1)
        else:
            s = -k * step
            part = pltpu.roll(jnp.where(at >= width - s, low, mid), s, mid.ndim - 1)
        part = part * tap
        total = part if total is None else total + part
    return total


UNROLL = {"stage": 16, "z": 4, "source": 4, "corr": 4, "sub": 4, "x": 1}


def loop(name, n, body, init):
    width = min(UNROLL[name], n)
    if n % width:
        width = 1
    if width == n:
        for i in range(n):
            init = body(i, init)
        return init

    def step(j, carry):
        for k in range(width):
            carry = body(j * width + k, carry)
        return carry

    return lax.fori_loop(0, n // width, step, init)


def turn(value, shift):
    return value if isinstance(shift, int) and shift == 0 else pltpu.roll(value, shift, 1)


def modulo(a, n):
    return a % n if isinstance(a, int) else lax.rem(a, n)


def kernel(sizes, w_ref, wave_ref, ext_ref, out_ref, corr_ref,
           wb, sb, xc, yb, pyb, psi, va, pack, zin, sums, sums2,
           send, recv, send2, recv2):
    nx, ny, nz = sizes
    cx, cy, cz = wave_ref.shape
    ix, iy, iz = (lax.axis_index(a) for a in AXES)
    plane = nx * nz
    per = cz // cx
    here = ix * nz + iz

    def plane_id(d):
        t = lax.rem(here + d, plane)
        return t, {"gx": lax.div(t, nz), "gz": lax.rem(t, nz)}

    def line_id(d):
        t = lax.rem(iy + d, ny)
        return t, {"gy": t}

    barrier = pltpu.get_barrier_semaphore()

    def greet(ids):
        def body(d, c):
            pl.semaphore_signal(barrier, inc=1, device_id=ids(d)[1], device_id_type=MESH)
            return c
        return body

    lax.fori_loop(1, plane, greet(plane_id), 0)
    lax.fori_loop(1, ny, greet(line_id), 0)

    counter = [0]

    def message(src, dst, dx, dy, dz):
        k = counter[0]
        counter[0] += 1
        to, back = None, None
        for d, i, n in ((dx, ix, nx), (dy, iy, ny), (dz, iz, nz)):
            if d > 0:
                a, b = i < n - 1, i > 0
            elif d < 0:
                a, b = i > 0, i < n - 1
            else:
                continue
            to = a if to is None else to & a
            back = b if back is None else back & b
        target = {}
        for name, d, i, n in zip(AXES, (dx, dy, dz), (ix, iy, iz), sizes):
            if d:
                target[name] = jnp.clip(i + d, 0, n - 1)
        copy = pltpu.make_async_remote_copy(
            src_ref=src, dst_ref=dst, send_sem=send.at[k], recv_sem=recv.at[k],
            device_id=target, device_id_type=MESH)
        return copy, to, back, dst

    sent = []

    def start(messages):
        for copy, to, _, _ in messages:
            pl.when(to)(copy.start)
            sent.append((copy, to))

    def blank(messages):
        for _, _, back, dst in messages:
            @pl.when(jnp.logical_not(back))
            def _(dst=dst):
                dst[...] = jnp.zeros(dst.shape, dst.dtype)

    def arrive(messages):
        for copy, _, back, _ in messages:
            pl.when(back)(copy.wait_recv)

    at = lanes((cy, cz))
    zero = jnp.zeros((cy, cz), jnp.float32)

    def pack_one(i, value, packs):
        mine = (at >= per * i) & (at < per * i + per)
        low = turn(value, per * i)
        high = turn(value, modulo(per * i + per, cz))
        return jnp.where(mine, low, packs[0]), jnp.where(mine, high, packs[1])

    def unpack(i, from_low, from_high):
        a = turn(from_high, modulo(cz - per * i, cz))
        b = turn(from_low, cz - per - per * i)
        return jnp.where(at < per, a, b)

    def pack_out(slot, packs):
        pack[slot, 0] = packs[0]
        pack[slot, 1] = packs[1]

    def z_messages(slot, across):
        out = []
        for dx in ((-1, 0, 1) if across else (0,)):
            out.append(message(pack.at[slot, 1], zin.at[slot, 0, 1 - dx], dx, 0, 1))
            out.append(message(pack.at[slot, 0], zin.at[slot, 1, 1 - dx], dx, 0, -1))
        return out

    def stage(i, packs):
        value = wave_ref[i]
        wb[R + i, pl.ds(R, cy)] = value
        return pack_one(i, value, packs)

    pack_out(0, loop("stage", cx, stage, (zero, zero)))

    wave_x = [
        message(wave_ref.at[pl.ds(cx - R, R)], wb.at[pl.ds(0, R), pl.ds(R, cy)], 1, 0, 0),
        message(wave_ref.at[pl.ds(0, R)], wb.at[pl.ds(R + cx, R), pl.ds(R, cy)], -1, 0, 0),
    ]
    wave_z = z_messages(0, True)
    wave_y = [
        message(wave_ref.at[:, pl.ds(cy - R, R)], wb.at[pl.ds(R, cx), pl.ds(0, R)], 0, 1, 0),
        message(wave_ref.at[:, pl.ds(0, R)], wb.at[pl.ds(R, cx), pl.ds(R + cy, R)], 0, -1, 0),
    ]

    def y_messages(buf):
        return [
            message(buf.at[:, pl.ds(cy, R)], buf.at[:, pl.ds(0, R)], 0, 1, 0),
            message(buf.at[:, pl.ds(R, R)], buf.at[:, pl.ds(R + cy, R)], 0, -1, 0),
        ]

    mid_y = y_messages(yb.at[0])
    src_x = [
        message(sb.at[pl.ds(cx, R)], sb.at[pl.ds(0, R)], 1, 0, 0),
        message(sb.at[pl.ds(R, R)], sb.at[pl.ds(R + cx, R)], -1, 0, 0),
    ]
    src_z = z_messages(1, True)
    end_y = y_messages(yb.at[1])

    psi_moves = []
    for s in range(SUBSTEPS - 1):
        buf = psi.at[s]
        moves = [
            message(buf.at[pl.ds(cx, H), pl.ds(R, cy)], buf.at[pl.ds(0, H), pl.ds(R, cy)], 1, 0, 0),
            message(buf.at[pl.ds(H, H), pl.ds(R, cy)], buf.at[pl.ds(H + cx, H), pl.ds(R, cy)], -1, 0, 0),
        ]
        own = pl.ds(H, cx)
        moves += [
            message(buf.at[own, pl.ds(cy, R)], buf.at[own, pl.ds(0, R)], 0, 1, 0),
            message(buf.at[own, pl.ds(R, R)], buf.at[own, pl.ds(R + cy, R)], 0, -1, 0),
        ]
        moves += z_messages(2 + s, False)
        psi_moves.append(moves)

    pl.semaphore_wait(barrier, plane - 1 + ny - 1)
    start(wave_x + wave_z + wave_y)
    for group in [wave_x, wave_z, wave_y, mid_y, src_x, src_z, end_y] + psi_moves:
        blank(group)

    def taps_of(dim, flip):
        return [(k, w_ref[dim, R - k if flip else R + k]) for k in range(-R, R + 1)]

    def smear_xz(src, y_at, slot, square, flip, buf):
        taps = taps_of(0, flip)

        def x_pass(j, c):
            rows = pl.ds(pl.multiple_of(y_at + 8 * j, 8), 8)
            ins = [src[k, rows] for k in range(cx + 2 * R)]
            if square:
                ins = [v * v for v in ins]
            for i in range(cx):
                total = None
                for k, tap in taps:
                    part = ins[i + R + k] * tap
                    total = part if total is None else total + part
                xc[i, pl.ds(pl.multiple_of(8 * j, 8), 8)] = total
            return c

        loop("x", cy // 8, x_pass, 0)
        sides = []
        for side in range(2):
            near = [zin[slot, side, place] for place in range(3)]
            if square:
                near = [v * v for v in near]
            sides.append(near)
        below = lane_taps(sides[0][1], sides[0][0], sides[0][2], per, taps)
        above = lane_taps(sides[1][1], sides[1][0], sides[1][2], per, taps)
        taps_z = taps_of(2, flip)

        def z_pass(i, c):
            near = unpack(i, below, above)
            buf[i, pl.ds(R, cy)] = lane_taps(xc[i], near, near, 1, taps_z)
            return c

        loop("z", cx, z_pass, 0)

    def smear_y(buf, i, taps):
        total = None
        for k, tap in taps:
            part = buf[i, pl.ds(R + k, cy)] * tap
            total = part if total is None else total + part
        return total

    arrive(wave_x + wave_z)
    smear_xz(wb, R, 0, True, False, yb.at[0])
    start(mid_y)
    arrive(mid_y)
    taps_y = taps_of(1, False)

    def source_pass(i, packs):
        coarse = smear_y(yb.at[0], i, taps_y)
        value = wave_ref[i]
        dens = value * value
        both = coarse * coarse
        source = 0.5 * dens * both - dens * coarse
        corr_ref[i] = (0.5 / 3.0) * both * coarse - 0.5 * both
        sb[R + i] = source
        return pack_one(i, source, packs)

    pack_out(1, loop("source", cx, source_pass, (zero, zero)))

    start(src_x + src_z)
    arrive(src_x + src_z)
    smear_xz(sb, 0, 1, False, True, yb.at[1])
    start(end_y)
    arrive(end_y)
    taps_yt = taps_of(1, True)

    def corr_pass(i, c):
        corr = corr_ref[i] + smear_y(yb.at[1], i, taps_yt)
        corr_ref[i] = corr
        va[i] = (1.0 + STEP * 0.5 * 3.0 * LAP_COEF[0]) - STEP * (corr + ext_ref[i])
        return c

    loop("corr", cx, corr_pass, 0)

    gains = [STEP * 0.5 * c for c in LAP_COEF]

    def advance(buf, reach, i, below, above):
        center = buf[reach + i, pl.ds(R, cy)]
        near = unpack(i, below, above)
        total = center * va[i]
        for k in range(1, H + 1):
            pair = buf[reach + i + k, pl.ds(R, cy)] + buf[reach + i - k, pl.ds(R, cy)]
            pair += buf[reach + i, pl.ds(R + k, cy)] + buf[reach + i, pl.ds(R - k, cy)]
            pair += pltpu.roll(jnp.where(at < k, near, center), cz - k, 1)
            pair += pltpu.roll(jnp.where(at >= cz - k, near, center), k, 1)
            total += gains[k] * pair
        return total

    arrive(wave_y)
    buf, reach, slot = wb, R, 0
    for s in range(SUBSTEPS):
        if s:
            arrive(psi_moves[s - 1])
        below, above = zin[slot, 0, 1], zin[slot, 1, 1]
        if s < SUBSTEPS - 1:
            after = psi.at[s]

            def middle(i, packs, buf=buf, reach=reach, below=below, above=above, after=after):
                value = advance(buf, reach, i, below, above)
                after[H + i, pl.ds(R, cy)] = value
                return pack_one(i, value, packs)

            pack_out(2 + s, loop("sub", cx, middle, (zero, zero)))
            start(psi_moves[s])
            buf, reach, slot = after, H, 2 + s
        else:
            def last(i, total):
                value = advance(buf, reach, i, below, above)
                out_ref[i] = value
                return total + value * value

            total = loop("sub", cx, last, zero)

    part = total[0:8]
    for j in range(1, cy // 8):
        part = part + total[8 * j:8 * j + 8]

    def all_sum(part, slots, ssem, rsem, me, n, ids):
        if n == 1:
            return part
        slots[n] = part

        def copy_of(d, slot):
            return pltpu.make_async_remote_copy(
                src_ref=slots.at[n], dst_ref=slots.at[slot], send_sem=ssem.at[d], recv_sem=rsem.at[slot],
                device_id=ids(d)[1], device_id_type=MESH)

        def go(d, c):
            copy_of(d, me).start()
            return c

        def come(d, c):
            t = ids(d)[0]
            copy_of(d, t).wait_recv()
            return c + slots[t]

        def left(d, c):
            copy_of(d, me).wait_send()
            return c

        lax.fori_loop(1, n, go, 0)
        total = lax.fori_loop(1, n, come, part)
        lax.fori_loop(1, n, left, 0)
        return total

    part = all_sum(part, sums, send2.at[0], recv2.at[0], here, plane, plane_id)
    part = all_sum(part, sums2, send2.at[1], recv2.at[1], iy, ny, line_id)
    cells = float(cx * cy * cz * nx * ny * nz)
    scale = lax.rsqrt(jnp.full((1, cz), jnp.sum(part), jnp.float32) / cells + 1e-06)

    def finish(i, c):
        out_ref[i] = out_ref[i] * scale
        return c

    loop("corr", cx, finish, 0)
    for copy, to in sent:
        pl.when(to)(copy.wait_send)


def shards(sizes, wave, external, weights):
    cx, cy, cz = wave.shape
    nx, ny, nz = sizes
    f32 = jnp.float32
    n_messages = 36
    most = max(nx * nz, ny)
    vmem = pl.BlockSpec(memory_space=pltpu.VMEM)
    return pl.pallas_call(
        functools.partial(kernel, sizes),
        out_shape=(jax.ShapeDtypeStruct(wave.shape, f32), jax.ShapeDtypeStruct(wave.shape, f32)),
        in_specs=[pl.BlockSpec(memory_space=pltpu.SMEM), vmem, vmem],
        out_specs=(vmem, vmem),
        scratch_shapes=[
            pltpu.VMEM((cx + 2 * R, cy + 2 * R, cz), f32),
            pltpu.VMEM((cx + 2 * R, cy, cz), f32),
            pltpu.VMEM((cx, cy, cz), f32),
            pltpu.VMEM((2, cx, cy + 2 * R, cz), f32),
            pltpu.VMEM((8, cz), f32),
            pltpu.VMEM((SUBSTEPS - 1, cx + 2 * H, cy + 2 * R, cz), f32),
            pltpu.VMEM((cx, cy, cz), f32),
            pltpu.VMEM((SUBSTEPS + 1, 2, cy, cz), f32),
            pltpu.VMEM((SUBSTEPS + 1, 2, 3, cy, cz), f32),
            pltpu.VMEM((nx * nz + 1, 8, cz), f32),
            pltpu.VMEM((ny + 1, 8, cz), f32),
            pltpu.SemaphoreType.DMA((n_messages,)),
            pltpu.SemaphoreType.DMA((n_messages,)),
            pltpu.SemaphoreType.DMA((2, most)),
            pltpu.SemaphoreType.DMA((2, most)),
        ],
        compiler_params=pltpu.CompilerParams(collective_id=0, has_side_effects=True,
                                             vmem_limit_bytes=32 * 1024 * 1024),
    )(weights, wave, external)


def solution(mesh):
    sizes = tuple(mesh.shape[a] for a in AXES)
    spec = P(*AXES)
    return jax.shard_map(
        functools.partial(shards, sizes),
        mesh=mesh,
        in_specs=(spec, spec, P()),
        out_specs=(spec, spec),
        check_vma=False,
    )
```

```python
import functools

import jax
import jax.numpy as jnp
from jax import lax
from jax.experimental import pallas as pl
from jax.experimental.pallas import tpu as pltpu
from jax.sharding import PartitionSpec as P

SUBSTEPS = 3
LAP_COEF = (-205.0 / 72.0, 8.0 / 5.0, -1.0 / 5.0, 8.0 / 315.0, -1.0 / 560.0)
STEP = 0.08
AXES = ("gx", "gy", "gz")
MESH = pl.DeviceIdType.MESH
R = 8
H = 4


def lanes(shape):
    return lax.broadcasted_iota(jnp.int32, shape, len(shape) - 1)


def lane_taps(mid, low, high, step, taps):
    at = lanes(mid.shape)
    width = mid.shape[-1]
    total = None
    for k, tap in taps:
        if k == 0:
            part = mid
        elif k > 0:
            s = k * step
            part = pltpu.roll(jnp.where(at < s, high, mid), width - s, mid.ndim - 1)
        else:
            s = -k * step
            part = pltpu.roll(jnp.where(at >= width - s, low, mid), s, mid.ndim - 1)
        part = part * tap
        total = part if total is None else total + part
    return total


UNROLL = {"stage": 16, "z": 2, "source": 4, "corr": 4, "sub": 4, "x": 1}
ZW = 4


def loop(name, n, body, init):
    width = min(UNROLL[name], n)
    if n % width:
        width = 1
    if width == n:
        for i in range(n):
            init = body(i, init)
        return init

    def step(j, carry):
        for k in range(width):
            carry = body(j * width + k, carry)
        return carry

    return lax.fori_loop(0, n // width, step, init)


def turn(value, shift):
    return value if isinstance(shift, int) and shift == 0 else pltpu.roll(value, shift, 1)


def modulo(a, n):
    return a % n if isinstance(a, int) else lax.rem(a, n)


def kernel(sizes, w_hbm, wave_hbm, ext_hbm, out_ref, corr_ref, scale_ref,
           wb, sb, xc, yb, psi, va, pack, zin, ypack, yin, bands, ext_ref, w_ref, sums, sums2,
           send, recv, send2, recv2, local):
    nx, ny, nz = sizes
    cx, cy, cz = wave_hbm.shape
    wave_ref = wb.at[pl.ds(R, cx), pl.ds(R, cy)]
    get_wave = pltpu.make_async_copy(wave_hbm, wave_ref, local.at[0])
    get_ext = pltpu.make_async_copy(ext_hbm, ext_ref, local.at[1])
    get_weights = pltpu.make_async_copy(w_hbm, w_ref, local.at[2])
    get_wave.start()
    get_weights.start()
    ix, iy, iz = (lax.axis_index(a) for a in AXES)
    plane = nx * nz
    per = cz // cx
    here = ix * nz + iz

    def plane_id(d):
        t = lax.rem(here + d, plane)
        return t, {"gx": lax.div(t, nz), "gz": lax.rem(t, nz)}

    def line_id(d):
        t = lax.rem(iy + d, ny)
        return t, {"gy": t}

    barrier = pltpu.get_barrier_semaphore()

    def greet(ids):
        def body(d, c):
            pl.semaphore_signal(barrier, inc=1, device_id=ids(d)[1], device_id_type=MESH)
            return c
        return body

    lax.fori_loop(1, plane, greet(plane_id), 0)
    lax.fori_loop(1, ny, greet(line_id), 0)

    counter = [0]

    def message(src, dst, dx, dy, dz):
        k = counter[0]
        counter[0] += 1
        to, back = None, None
        for d, i, n in ((dx, ix, nx), (dy, iy, ny), (dz, iz, nz)):
            if d > 0:
                a, b = i < n - 1, i > 0
            elif d < 0:
                a, b = i > 0, i < n - 1
            else:
                continue
            to = a if to is None else to & a
            back = b if back is None else back & b
        target = {}
        for name, d, i, n in zip(AXES, (dx, dy, dz), (ix, iy, iz), sizes):
            if d:
                target[name] = jnp.clip(i + d, 0, n - 1)
        copy = pltpu.make_async_remote_copy(
            src_ref=src, dst_ref=dst, send_sem=send.at[k], recv_sem=recv.at[k],
            device_id=target, device_id_type=MESH)
        return copy, to, back, dst

    sent = []

    def start(messages):
        for copy, to, _, _ in messages:
            pl.when(to)(copy.start)
            sent.append((copy, to))

    def blank(messages):
        for _, _, back, dst in messages:
            @pl.when(jnp.logical_not(back))
            def _(dst=dst):
                dst[...] = jnp.zeros(dst.shape, dst.dtype)

    def arrive(messages):
        for copy, _, back, _ in messages:
            pl.when(back)(copy.wait_recv)

    at = lanes((cy, cz))
    zero = jnp.zeros((cy, cz), jnp.float32)

    def pack_one(i, value, packs):
        mine = (at >= per * i) & (at < per * i + per)
        low = turn(value, per * i)
        high = turn(value, modulo(per * i + per, cz))
        return jnp.where(mine, low, packs[0]), jnp.where(mine, high, packs[1])

    def unpack(i, from_low, from_high):
        a = turn(from_high, modulo(cz - per * i, cz))
        b = turn(from_low, cz - per - per * i)
        return jnp.where(at < per, a, b)

    def pack_out(slot, packs):
        pack[slot, 0] = packs[0]
        pack[slot, 1] = packs[1]

    def z_messages(slot, across):
        out = []
        for dx in ((-1, 0, 1) if across else (0,)):
            out.append(message(pack.at[slot, 1], zin.at[slot, 0, 1 - dx], dx, 0, 1))
            out.append(message(pack.at[slot, 0], zin.at[slot, 1, 1 - dx], dx, 0, -1))
        return out

    def stage(i, packs):
        return pack_one(i, wave_ref[i], packs)

    get_wave.wait()

    pack_out(0, loop("stage", cx, stage, (zero, zero)))

    wave_x = [
        message(wave_ref.at[pl.ds(cx - R, R)], wb.at[pl.ds(0, R), pl.ds(R, cy)], 1, 0, 0),
        message(wave_ref.at[pl.ds(0, R)], wb.at[pl.ds(R + cx, R), pl.ds(R, cy)], -1, 0, 0),
    ]
    wave_z = z_messages(0, True)
    wave_y = [
        message(wave_ref.at[:, pl.ds(cy - R, R)], wb.at[pl.ds(R, cx), pl.ds(0, R)], 0, 1, 0),
        message(wave_ref.at[:, pl.ds(0, R)], wb.at[pl.ds(R, cx), pl.ds(R + cy, R)], 0, -1, 0),
    ]

    def y_messages(buf):
        return [
            message(buf.at[:, pl.ds(cy, R)], buf.at[:, pl.ds(0, R)], 0, 1, 0),
            message(buf.at[:, pl.ds(R, R)], buf.at[:, pl.ds(R + cy, R)], 0, -1, 0),
        ]

    mid_y = y_messages(yb.at[0])
    src_x = [
        message(sb.at[pl.ds(cx, R)], sb.at[pl.ds(0, R)], 1, 0, 0),
        message(sb.at[pl.ds(R, R)], sb.at[pl.ds(R + cx, R)], -1, 0, 0),
    ]
    src_z = z_messages(1, True)
    end_y = y_messages(yb.at[1])

    psi_moves = []
    for s in range(SUBSTEPS - 1):
        buf = psi.at[s]
        moves = [
            message(buf.at[pl.ds(cx, H), pl.ds(R, cy)], buf.at[pl.ds(0, H), pl.ds(R, cy)], 1, 0, 0),
            message(buf.at[pl.ds(H, H), pl.ds(R, cy)], buf.at[pl.ds(H + cx, H), pl.ds(R, cy)], -1, 0, 0),
        ]
        moves += [
            message(ypack.at[s, 1], yin.at[s, 0], 0, 1, 0),
            message(ypack.at[s, 0], yin.at[s, 1], 0, -1, 0),
        ]
        moves += z_messages(2 + s, False)
        psi_moves.append(moves)

    pl.semaphore_wait(barrier, plane - 1 + ny - 1)
    start(wave_x + wave_z + wave_y)
    get_ext.start()
    get_weights.wait()
    for group in [wave_x, wave_z, wave_y, mid_y, src_x, src_z, end_y] + psi_moves:
        blank(group)

    def taps_of(dim, flip):
        return [(k, w_ref[dim, R - k if flip else R + k]) for k in range(-R, R + 1)]

    row = lax.broadcasted_iota(jnp.int32, (cz, cz), 0)
    gap = row - lanes((cz, cz))

    def band(slot, taps):
        inner = jnp.zeros((cz, cz), jnp.float32)
        outer = inner
        for k, tap in taps:
            inner = jnp.where(gap == k, tap, inner)
            if k:
                outer = jnp.where(gap == (k - cz if k > 0 else k + cz), tap, outer)
        bands[slot, pl.ds(0, cz)] = inner
        bands[slot, pl.ds(cz, cz)] = outer

    def along_z(values, nears, slot):
        both = jnp.concatenate([jnp.concatenate(values, 0), jnp.concatenate(nears, 0)], 1)
        return jnp.dot(both, bands[slot], precision=lax.Precision.HIGHEST,
                       preferred_element_type=jnp.float32)

    band(0, taps_of(2, False))
    band(1, taps_of(2, True))

    def smear_xz(src, y_at, slot, square, flip, buf):
        taps = taps_of(0, flip)

        def x_pass(j, c):
            rows = pl.ds(pl.multiple_of(y_at + 8 * j, 8), 8)
            ins = [src[k, rows] for k in range(cx + 2 * R)]
            if square:
                ins = [v * v for v in ins]
            for i in range(cx):
                total = None
                for k, tap in taps:
                    part = ins[i + R + k] * tap
                    total = part if total is None else total + part
                xc[i, pl.ds(pl.multiple_of(8 * j, 8), 8)] = total
            return c

        loop("x", cy // 8, x_pass, 0)
        sides = []
        for side in range(2):
            near = [zin[slot, side, place] for place in range(3)]
            if square:
                near = [v * v for v in near]
            sides.append(near)
        below = lane_taps(sides[0][1], sides[0][0], sides[0][2], per, taps)
        above = lane_taps(sides[1][1], sides[1][0], sides[1][2], per, taps)

        def z_pass(group, c):
            these = [group * ZW + k for k in range(ZW)]
            made = along_z([xc[i] for i in these], [unpack(i, below, above) for i in these], int(flip))
            for k, i in enumerate(these):
                buf[i, pl.ds(R, cy)] = made[k * cy:(k + 1) * cy]
            return c

        loop("z", cx // ZW, z_pass, 0)

    def smear_y(buf, i, taps):
        total = None
        for k, tap in taps:
            part = buf[i, pl.ds(R + k, cy)] * tap
            total = part if total is None else total + part
        return total

    arrive(wave_x + wave_z)
    smear_xz(wb, R, 0, True, False, yb.at[0])
    start(mid_y)
    arrive(mid_y)
    taps_y = taps_of(1, False)

    def source_pass(i, packs):
        coarse = smear_y(yb.at[0], i, taps_y)
        value = wave_ref[i]
        dens = value * value
        both = coarse * coarse
        source = 0.5 * dens * both - dens * coarse
        corr_ref[i] = (0.5 / 3.0) * both * coarse - 0.5 * both
        sb[R + i] = source
        return pack_one(i, source, packs)

    pack_out(1, loop("source", cx, source_pass, (zero, zero)))

    start(src_x + src_z)
    arrive(src_x + src_z)
    smear_xz(sb, 0, 1, False, True, yb.at[1])
    start(end_y)
    arrive(end_y)
    taps_yt = taps_of(1, True)

    get_ext.wait()

    def corr_pass(i, c):
        corr = corr_ref[i] + smear_y(yb.at[1], i, taps_yt)
        corr_ref[i] = corr
        va[i] = (1.0 + STEP * 0.5 * 3.0 * LAP_COEF[0]) - STEP * (corr + ext_ref[i])
        return c

    loop("corr", cx, corr_pass, 0)

    gains = [STEP * 0.5 * c for c in LAP_COEF]

    def advance(buf, reach, i, below, above):
        center = buf[reach + i, pl.ds(R, cy)]
        near = unpack(i, below, above)
        total = center * va[i]
        for k in range(1, H + 1):
            pair = buf[reach + i + k, pl.ds(R, cy)] + buf[reach + i - k, pl.ds(R, cy)]
            pair += buf[reach + i, pl.ds(R + k, cy)] + buf[reach + i, pl.ds(R - k, cy)]
            pair += pltpu.roll(jnp.where(at < k, near, center), cz - k, 1)
            pair += pltpu.roll(jnp.where(at >= cz - k, near, center), k, 1)
            total += gains[k] * pair
        return total

    arrive(wave_y)
    buf, reach, slot = wb, R, 0
    for s in range(SUBSTEPS):
        if s:
            arrive(psi_moves[s - 1])
            for i in range(cx):
                half = pl.ds(H * (i % 2), H)
                buf[H + i, pl.ds(R - H, H)] = yin[s - 1, 0, i // 2, half]
                buf[H + i, pl.ds(R + cy, H)] = yin[s - 1, 1, i // 2, half]
        below, above = zin[slot, 0, 1], zin[slot, 1, 1]
        if s < SUBSTEPS - 1:
            after = psi.at[s]

            def middle(i, packs, buf=buf, reach=reach, below=below, above=above, after=after):
                value = advance(buf, reach, i, below, above)
                after[H + i, pl.ds(R, cy)] = value
                return pack_one(i, value, packs)

            pack_out(2 + s, loop("sub", cx, middle, (zero, zero)))
            for i in range(cx):
                half = pl.ds(H * (i % 2), H)
                ypack[s, 0, i // 2, half] = after[H + i, pl.ds(R, H)]
                ypack[s, 1, i // 2, half] = after[H + i, pl.ds(R + cy - H, H)]
            start(psi_moves[s])
            buf, reach, slot = after, H, 2 + s
        else:
            def last(i, total):
                value = advance(buf, reach, i, below, above)
                out_ref[i] = value
                return total + value * value

            total = loop("sub", cx, last, zero)

    part = total[0:8]
    for j in range(1, cy // 8):
        part = part + total[8 * j:8 * j + 8]

    def all_sum(part, slots, ssem, rsem, me, n, ids):
        if n == 1:
            return part
        slots[n] = part

        def copy_of(d, slot):
            return pltpu.make_async_remote_copy(
                src_ref=slots.at[n], dst_ref=slots.at[slot], send_sem=ssem.at[d], recv_sem=rsem.at[slot],
                device_id=ids(d)[1], device_id_type=MESH)

        def go(d, c):
            copy_of(d, me).start()
            return c

        def come(d, c):
            t = ids(d)[0]
            copy_of(d, t).wait_recv()
            return c + slots[t]

        def left(d, c):
            copy_of(d, me).wait_send()
            return c

        lax.fori_loop(1, n, go, 0)
        total = lax.fori_loop(1, n, come, part)
        lax.fori_loop(1, n, left, 0)
        return total

    part = all_sum(part, sums, send2.at[0], recv2.at[0], here, plane, plane_id)
    part = all_sum(part, sums2, send2.at[1], recv2.at[1], iy, ny, line_id)
    cells = float(cx * cy * cz * nx * ny * nz)
    scale_ref[...] = lax.rsqrt(jnp.full(scale_ref.shape, jnp.sum(part), jnp.float32) / cells + 1e-06)
    for copy, to in sent:
        pl.when(to)(copy.wait_send)


def shards(sizes, wave, external, weights):
    cx, cy, cz = wave.shape
    nx, ny, nz = sizes
    f32 = jnp.float32
    n_messages = 36
    most = max(nx * nz, ny)
    vmem = pl.BlockSpec(memory_space=pltpu.VMEM)
    stay = pl.BlockSpec(memory_space=pltpu.HBM)
    psi, corr, scale = pl.pallas_call(
        functools.partial(kernel, sizes),
        out_shape=(jax.ShapeDtypeStruct(wave.shape, f32), jax.ShapeDtypeStruct(wave.shape, f32),
                   jax.ShapeDtypeStruct((8, cz), f32)),
        in_specs=[stay, stay, stay],
        out_specs=(vmem, vmem, vmem),
        scratch_shapes=[
            pltpu.VMEM((cx + 2 * R, cy + 2 * R, cz), f32),
            pltpu.VMEM((cx + 2 * R, cy, cz), f32),
            pltpu.VMEM((cx, cy, cz), f32),
            pltpu.VMEM((2, cx, cy + 2 * R, cz), f32),
            pltpu.VMEM((SUBSTEPS - 1, cx + 2 * H, cy + 2 * R, cz), f32),
            pltpu.VMEM((cx, cy, cz), f32),
            pltpu.VMEM((SUBSTEPS + 1, 2, cy, cz), f32),
            pltpu.VMEM((SUBSTEPS + 1, 2, 3, cy, cz), f32),
            pltpu.VMEM((SUBSTEPS - 1, 2, cx // 2, 2 * H, cz), f32),
            pltpu.VMEM((SUBSTEPS - 1, 2, cx // 2, 2 * H, cz), f32),
            pltpu.VMEM((2, 2 * cz, cz), f32),
            pltpu.VMEM((cx, cy, cz), f32),
            pltpu.SMEM(weights.shape, f32),
            pltpu.VMEM((nx * nz + 1, 8, cz), f32),
            pltpu.VMEM((ny + 1, 8, cz), f32),
            pltpu.SemaphoreType.DMA((n_messages,)),
            pltpu.SemaphoreType.DMA((n_messages,)),
            pltpu.SemaphoreType.DMA((2, most)),
            pltpu.SemaphoreType.DMA((2, most)),
            pltpu.SemaphoreType.DMA((3,)),
        ],
        compiler_params=pltpu.CompilerParams(collective_id=0, has_side_effects=True,
                                             vmem_limit_bytes=67043328),
    )(weights, wave, external)
    return psi * scale[0, 0], corr


def solution(mesh):
    sizes = tuple(mesh.shape[a] for a in AXES)
    spec = P(*AXES)
    return jax.shard_map(
        functools.partial(shards, sizes),
        mesh=mesh,
        in_specs=(spec, spec, P()),
        out_specs=(spec, spec),
        check_vma=False,
    )
```

```python
import functools

import jax
import jax.numpy as jnp
from jax import lax
from jax.experimental import pallas as pl
from jax.experimental.pallas import tpu as pltpu
from jax.sharding import PartitionSpec as P

SUBSTEPS = 3
LAP_COEF = (-205.0 / 72.0, 8.0 / 5.0, -1.0 / 5.0, 8.0 / 315.0, -1.0 / 560.0)
STEP = 0.08
AXES = ("gx", "gy", "gz")
MESH = pl.DeviceIdType.MESH
R = 8
H = 4


def lanes(shape):
    return lax.broadcasted_iota(jnp.int32, shape, len(shape) - 1)


def lane_taps(mid, low, high, step, taps):
    at = lanes(mid.shape)
    width = mid.shape[-1]
    total = None
    for k, tap in taps:
        if k == 0:
            part = mid
        elif k > 0:
            s = k * step
            part = pltpu.roll(jnp.where(at < s, high, mid), width - s, mid.ndim - 1)
        else:
            s = -k * step
            part = pltpu.roll(jnp.where(at >= width - s, low, mid), s, mid.ndim - 1)
        part = part * tap
        total = part if total is None else total + part
    return total


PARTNERS = [(dx, 0, dz) for dx in (-1, 0, 1) for dz in (-1, 0, 1) if dx or dz] + [(0, 1, 0), (0, -1, 0)]
UNROLL = {"stage": 16, "z": 2, "source": 4, "corr": 4, "sub": 4, "x": 1}
ZW = 4


def loop(name, n, body, init):
    width = min(UNROLL[name], n)
    if n % width:
        width = 1
    if width == n:
        for i in range(n):
            init = body(i, init)
        return init

    def step(j, carry):
        for k in range(width):
            carry = body(j * width + k, carry)
        return carry

    return lax.fori_loop(0, n // width, step, init)


def turn(value, shift):
    return value if isinstance(shift, int) and shift == 0 else pltpu.roll(value, shift, 1)


def modulo(a, n):
    return a % n if isinstance(a, int) else lax.rem(a, n)


def kernel(sizes, w_hbm, wave_hbm, ext_hbm, out_ref, corr_ref, scale_ref,
           wb, sb, xc, yb, psi, va, pack, zin, ypack, yin, bands, ext_ref, w_ref, sums, sums2,
           send, recv, send2, recv2, local):
    nx, ny, nz = sizes
    cx, cy, cz = wave_hbm.shape
    wave_ref = wb.at[pl.ds(R, cx), pl.ds(R, cy)]
    get_wave = pltpu.make_async_copy(wave_hbm, wave_ref, local.at[0])
    get_ext = pltpu.make_async_copy(ext_hbm, ext_ref, local.at[1])
    get_weights = pltpu.make_async_copy(w_hbm, w_ref, local.at[2])
    get_wave.start()
    get_weights.start()
    ix, iy, iz = (lax.axis_index(a) for a in AXES)
    plane = nx * nz
    per = cz // cx
    here = ix * nz + iz

    def plane_id(d):
        t = lax.rem(here + d, plane)
        return t, {"gx": lax.div(t, nz), "gz": lax.rem(t, nz)}

    def line_id(d):
        t = lax.rem(iy + d, ny)
        return t, {"gy": t}

    barrier = pltpu.get_barrier_semaphore()

    def greet(ids):
        def body(d, c):
            pl.semaphore_signal(barrier, inc=1, device_id=ids(d)[1], device_id_type=MESH)
            return c
        return body

    near = nx <= 4 and ny <= 4 and nz <= 2
    if near:
        guests = 0
        for dx, dy, dz in PARTNERS:
            there = None
            target = {}
            for name, d, i, n in zip(AXES, (dx, dy, dz), (ix, iy, iz), sizes):
                if d:
                    ok = i < n - 1 if d > 0 else i > 0
                    there = ok if there is None else there & ok
                    target[name] = jnp.clip(i + d, 0, n - 1)
            guests += there.astype(jnp.int32)

            @pl.when(there)
            def _(target=target):
                pl.semaphore_signal(barrier, inc=1, device_id=target, device_id_type=MESH)
    else:
        guests = plane - 1 + ny - 1
        lax.fori_loop(1, plane, greet(plane_id), 0)
        lax.fori_loop(1, ny, greet(line_id), 0)

    counter = [0]

    def message(src, dst, dx, dy, dz):
        k = counter[0]
        counter[0] += 1
        to, back = None, None
        for d, i, n in ((dx, ix, nx), (dy, iy, ny), (dz, iz, nz)):
            if d > 0:
                a, b = i < n - 1, i > 0
            elif d < 0:
                a, b = i > 0, i < n - 1
            else:
                continue
            to = a if to is None else to & a
            back = b if back is None else back & b
        target = {}
        for name, d, i, n in zip(AXES, (dx, dy, dz), (ix, iy, iz), sizes):
            if d:
                target[name] = jnp.clip(i + d, 0, n - 1)
        copy = pltpu.make_async_remote_copy(
            src_ref=src, dst_ref=dst, send_sem=send.at[k], recv_sem=recv.at[k],
            device_id=target, device_id_type=MESH)
        return copy, to, back, dst

    sent = []

    def start(messages):
        for copy, to, _, _ in messages:
            pl.when(to)(copy.start)
            sent.append((copy, to))

    def blank(messages):
        for _, _, back, dst in messages:
            @pl.when(jnp.logical_not(back))
            def _(dst=dst):
                dst[...] = jnp.zeros(dst.shape, dst.dtype)

    def arrive(messages):
        for copy, _, back, _ in messages:
            pl.when(back)(copy.wait_recv)

    at = lanes((cy, cz))
    zero = jnp.zeros((cy, cz), jnp.float32)

    def pack_one(i, value, packs):
        mine = (at >= per * i) & (at < per * i + per)
        low = turn(value, per * i)
        high = turn(value, modulo(per * i + per, cz))
        return jnp.where(mine, low, packs[0]), jnp.where(mine, high, packs[1])

    def unpack(i, from_low, from_high):
        a = turn(from_high, modulo(cz - per * i, cz))
        b = turn(from_low, cz - per - per * i)
        return jnp.where(at < per, a, b)

    def pack_out(slot, packs):
        pack[slot, 0] = packs[0]
        pack[slot, 1] = packs[1]

    def z_messages(slot, across):
        out = []
        for dx in ((-1, 0, 1) if across else (0,)):
            out.append(message(pack.at[slot, 1], zin.at[slot, 0, 1 - dx], dx, 0, 1))
            out.append(message(pack.at[slot, 0], zin.at[slot, 1, 1 - dx], dx, 0, -1))
        return out

    def stage(i, packs):
        return pack_one(i, wave_ref[i], packs)

    get_wave.wait()

    pack_out(0, loop("stage", cx, stage, (zero, zero)))

    wave_x = [
        message(wave_ref.at[pl.ds(cx - R, R)], wb.at[pl.ds(0, R), pl.ds(R, cy)], 1, 0, 0),
        message(wave_ref.at[pl.ds(0, R)], wb.at[pl.ds(R + cx, R), pl.ds(R, cy)], -1, 0, 0),
    ]
    wave_z = z_messages(0, True)
    wave_y = [
        message(wave_ref.at[:, pl.ds(cy - R, R)], wb.at[pl.ds(R, cx), pl.ds(0, R)], 0, 1, 0),
        message(wave_ref.at[:, pl.ds(0, R)], wb.at[pl.ds(R, cx), pl.ds(R + cy, R)], 0, -1, 0),
    ]

    def y_messages(buf):
        return [
            message(buf.at[:, pl.ds(cy, R)], buf.at[:, pl.ds(0, R)], 0, 1, 0),
            message(buf.at[:, pl.ds(R, R)], buf.at[:, pl.ds(R + cy, R)], 0, -1, 0),
        ]

    mid_y = y_messages(yb.at[0])
    src_x = [
        message(sb.at[pl.ds(cx, R)], sb.at[pl.ds(0, R)], 1, 0, 0),
        message(sb.at[pl.ds(R, R)], sb.at[pl.ds(R + cx, R)], -1, 0, 0),
    ]
    src_z = z_messages(1, True)
    end_y = y_messages(yb.at[1])

    psi_moves = []
    for s in range(SUBSTEPS - 1):
        buf = psi.at[s]
        moves = [
            message(buf.at[pl.ds(cx, H), pl.ds(R, cy)], buf.at[pl.ds(0, H), pl.ds(R, cy)], 1, 0, 0),
            message(buf.at[pl.ds(H, H), pl.ds(R, cy)], buf.at[pl.ds(H + cx, H), pl.ds(R, cy)], -1, 0, 0),
        ]
        moves += [
            message(ypack.at[s, 1], yin.at[s, 0], 0, 1, 0),
            message(ypack.at[s, 0], yin.at[s, 1], 0, -1, 0),
        ]
        moves += z_messages(2 + s, False)
        psi_moves.append(moves)

    pl.semaphore_wait(barrier, guests)
    start(wave_x + wave_z + wave_y)
    get_ext.start()
    get_weights.wait()
    for group in [wave_x, wave_z, wave_y, mid_y, src_x, src_z, end_y] + psi_moves:
        blank(group)

    def taps_of(dim, flip):
        return [(k, w_ref[dim, R - k if flip else R + k]) for k in range(-R, R + 1)]

    row = lax.broadcasted_iota(jnp.int32, (cz, cz), 0)
    gap = row - lanes((cz, cz))

    def band(slot, taps):
        inner = jnp.zeros((cz, cz), jnp.float32)
        outer = inner
        for k, tap in taps:
            inner = jnp.where(gap == k, tap, inner)
            if k:
                outer = jnp.where(gap == (k - cz if k > 0 else k + cz), tap, outer)
        bands[slot, pl.ds(0, cz)] = inner
        bands[slot, pl.ds(cz, cz)] = outer

    def along_z(values, nears, slot):
        both = jnp.concatenate([jnp.concatenate(values, 0), jnp.concatenate(nears, 0)], 1)
        return jnp.dot(both, bands[slot], precision=lax.Precision.HIGHEST,
                       preferred_element_type=jnp.float32)

    band(0, taps_of(2, False))
    band(1, taps_of(2, True))

    def smear_xz(src, y_at, slot, square, flip, buf):
        taps = taps_of(0, flip)

        def x_pass(j, c):
            rows = pl.ds(pl.multiple_of(y_at + 8 * j, 8), 8)
            ins = [src[k, rows] for k in range(cx + 2 * R)]
            if square:
                ins = [v * v for v in ins]
            for i in range(cx):
                total = None
                for k, tap in taps:
                    part = ins[i + R + k] * tap
                    total = part if total is None else total + part
                xc[i, pl.ds(pl.multiple_of(8 * j, 8), 8)] = total
            return c

        loop("x", cy // 8, x_pass, 0)
        sides = []
        for side in range(2):
            near = [zin[slot, side, place] for place in range(3)]
            if square:
                near = [v * v for v in near]
            sides.append(near)
        below = lane_taps(sides[0][1], sides[0][0], sides[0][2], per, taps)
        above = lane_taps(sides[1][1], sides[1][0], sides[1][2], per, taps)

        def z_pass(group, c):
            these = [group * ZW + k for k in range(ZW)]
            made = along_z([xc[i] for i in these], [unpack(i, below, above) for i in these], int(flip))
            for k, i in enumerate(these):
                buf[i, pl.ds(R, cy)] = made[k * cy:(k + 1) * cy]
            return c

        loop("z", cx // ZW, z_pass, 0)

    def smear_y(buf, i, taps):
        total = None
        for k, tap in taps:
            part = buf[i, pl.ds(R + k, cy)] * tap
            total = part if total is None else total + part
        return total

    arrive(wave_x + wave_z)
    smear_xz(wb, R, 0, True, False, yb.at[0])
    start(mid_y)
    arrive(mid_y)
    taps_y = taps_of(1, False)

    def source_pass(i, packs):
        coarse = smear_y(yb.at[0], i, taps_y)
        value = wave_ref[i]
        dens = value * value
        both = coarse * coarse
        source = 0.5 * dens * both - dens * coarse
        corr_ref[i] = (0.5 / 3.0) * both * coarse - 0.5 * both
        sb[R + i] = source
        return pack_one(i, source, packs)

    pack_out(1, loop("source", cx, source_pass, (zero, zero)))

    start(src_x + src_z)
    arrive(src_x + src_z)
    smear_xz(sb, 0, 1, False, True, yb.at[1])
    start(end_y)
    arrive(end_y)
    taps_yt = taps_of(1, True)

    get_ext.wait()

    def corr_pass(i, c):
        corr = corr_ref[i] + smear_y(yb.at[1], i, taps_yt)
        corr_ref[i] = corr
        va[i] = (1.0 + STEP * 0.5 * 3.0 * LAP_COEF[0]) - STEP * (corr + ext_ref[i])
        return c

    loop("corr", cx, corr_pass, 0)

    gains = [STEP * 0.5 * c for c in LAP_COEF]

    band(2, [(k, gains[abs(k)]) for k in range(-H, H + 1) if k])

    def advance(buf, reach, these, below, above):
        centers = [buf[reach + i, pl.ds(R, cy)] for i in these]
        along = along_z(centers, [unpack(i, below, above) for i in these], 2)
        made = []
        for at_, i in enumerate(these):
            total = centers[at_] * va[i] + along[at_ * cy:(at_ + 1) * cy]
            for k in range(1, H + 1):
                pair = buf[reach + i + k, pl.ds(R, cy)] + buf[reach + i - k, pl.ds(R, cy)]
                pair += buf[reach + i, pl.ds(R + k, cy)] + buf[reach + i, pl.ds(R - k, cy)]
                total += gains[k] * pair
            made.append(total)
        return made

    groups = [list(range(g, g + ZW)) for g in range(0, cx, ZW)]
    groups = groups[:1] + groups[-1:] + groups[1:-1]
    arrive(wave_y)
    buf, reach, slot = wb, R, 0
    for s in range(SUBSTEPS):
        if s:
            arrive(psi_moves[s - 1])
            for i in range(cx):
                half = pl.ds(H * (i % 2), H)
                buf[H + i, pl.ds(R - H, H)] = yin[s - 1, 0, i // 2, half]
                buf[H + i, pl.ds(R + cy, H)] = yin[s - 1, 1, i // 2, half]
        below, above = zin[slot, 0, 1], zin[slot, 1, 1]
        if s < SUBSTEPS - 1:
            after = psi.at[s]
            packs = (zero, zero)
            for n_, these in enumerate(groups):
                for i, value in zip(these, advance(buf, reach, these, below, above)):
                    after[H + i, pl.ds(R, cy)] = value
                    packs = pack_one(i, value, packs)
                    half = pl.ds(H * (i % 2), H)
                    ypack[s, 0, i // 2, half] = value[:H]
                    ypack[s, 1, i // 2, half] = value[cy - H:]
                if n_ == 1:
                    start(psi_moves[s][:2])
            pack_out(2 + s, packs)
            start(psi_moves[s][2:])
            buf, reach, slot = after, H, 2 + s
        else:
            total = zero
            for these in groups:
                for i, value in zip(these, advance(buf, reach, these, below, above)):
                    out_ref[i] = value
                    total = total + value * value

    part = jnp.sum(total, axis=0, keepdims=True)
    everyone = plane * ny
    me = iy * plane + here

    def any_id(d):
        t = lax.rem(me + d, everyone)
        p = lax.rem(t, plane)
        return t, {"gx": lax.div(p, nz), "gy": lax.div(t, plane), "gz": lax.rem(p, nz)}

    def all_sum(part, slots, ssem, rsem, me, n, ids):
        if n == 1:
            return part
        slots[me] = part

        def copy_of(d, slot):
            return pltpu.make_async_remote_copy(
                src_ref=slots.at[me], dst_ref=slots.at[slot], send_sem=ssem.at[d], recv_sem=rsem.at[slot],
                device_id=ids(d)[1], device_id_type=MESH)

        def go(d, c):
            copy_of(d, me).start()
            return c

        def come(d, c):
            copy_of(d, ids(d)[0]).wait_recv()
            return c

        def left(d, c):
            copy_of(d, me).wait_send()
            return c

        lax.fori_loop(1, n, go, 0)
        lax.fori_loop(1, n, come, 0)
        total = jnp.sum(slots[...], axis=0)
        lax.fori_loop(1, n, left, 0)
        return total

    if near:
        part = all_sum(part, sums, send2.at[0], recv2.at[0], me, everyone, any_id)
    else:
        part = all_sum(part, sums, send2.at[0], recv2.at[0], here, plane, plane_id)
        part = all_sum(part, sums2, send2.at[1], recv2.at[1], iy, ny, line_id)
    cells = float(cx * cy * cz * nx * ny * nz)
    scale_ref[...] = lax.rsqrt(jnp.full(scale_ref.shape, jnp.sum(part), jnp.float32) / cells + 1e-06)
    for copy, to in sent:
        pl.when(to)(copy.wait_send)


def shards(sizes, wave, external, weights):
    cx, cy, cz = wave.shape
    nx, ny, nz = sizes
    f32 = jnp.float32
    n_messages = 36
    summed = nx * ny * nz if nx <= 4 and ny <= 4 and nz <= 2 else nx * nz
    most = max(summed, ny)
    vmem = pl.BlockSpec(memory_space=pltpu.VMEM)
    stay = pl.BlockSpec(memory_space=pltpu.HBM)
    psi, corr, scale = pl.pallas_call(
        functools.partial(kernel, sizes),
        out_shape=(jax.ShapeDtypeStruct(wave.shape, f32), jax.ShapeDtypeStruct(wave.shape, f32),
                   jax.ShapeDtypeStruct((8, cz), f32)),
        in_specs=[stay, stay, stay],
        out_specs=(vmem, vmem, vmem),
        scratch_shapes=[
            pltpu.VMEM((cx + 2 * R, cy + 2 * R, cz), f32),
            pltpu.VMEM((cx + 2 * R, cy, cz), f32),
            pltpu.VMEM((cx, cy, cz), f32),
            pltpu.VMEM((2, cx, cy + 2 * R, cz), f32),
            pltpu.VMEM((SUBSTEPS - 1, cx + 2 * H, cy + 2 * R, cz), f32),
            pltpu.VMEM((cx, cy, cz), f32),
            pltpu.VMEM((SUBSTEPS + 1, 2, cy, cz), f32),
            pltpu.VMEM((SUBSTEPS + 1, 2, 3, cy, cz), f32),
            pltpu.VMEM((SUBSTEPS - 1, 2, cx // 2, 2 * H, cz), f32),
            pltpu.VMEM((SUBSTEPS - 1, 2, cx // 2, 2 * H, cz), f32),
            pltpu.VMEM((3, 2 * cz, cz), f32),
            pltpu.VMEM((cx, cy, cz), f32),
            pltpu.SMEM(weights.shape, f32),
            pltpu.VMEM((summed, 1, cz), f32),
            pltpu.VMEM((ny, 1, cz), f32),
            pltpu.SemaphoreType.DMA((n_messages,)),
            pltpu.SemaphoreType.DMA((n_messages,)),
            pltpu.SemaphoreType.DMA((2, most)),
            pltpu.SemaphoreType.DMA((2, most)),
            pltpu.SemaphoreType.DMA((3,)),
        ],
        compiler_params=pltpu.CompilerParams(collective_id=0, has_side_effects=True,
                                             vmem_limit_bytes=48 * 1024 * 1024),
    )(*[pltpu.with_memory_space_constraint(x, pltpu.HBM) for x in (weights, wave, external)])
    return psi * scale[0, 0], corr


def solution(mesh):
    sizes = tuple(mesh.shape[a] for a in AXES)
    spec = P(*AXES)
    return jax.shard_map(
        functools.partial(shards, sizes),
        mesh=mesh,
        in_specs=(spec, spec, P()),
        out_specs=(spec, spec),
        check_vma=False,
    )
```

```python
import functools

import jax
import jax.numpy as jnp
from jax import lax
from jax.experimental import pallas as pl
from jax.experimental.pallas import tpu as pltpu
from jax.sharding import PartitionSpec as P

SUBSTEPS = 3
LAP_COEF = (-205.0 / 72.0, 8.0 / 5.0, -1.0 / 5.0, 8.0 / 315.0, -1.0 / 560.0)
STEP = 0.08
AXES = ("gx", "gy", "gz")
MESH = pl.DeviceIdType.MESH
R = 8
H = 4


def lanes(shape):
    return lax.broadcasted_iota(jnp.int32, shape, len(shape) - 1)


def lane_taps(mid, low, high, step, taps):
    at = lanes(mid.shape)
    width = mid.shape[-1]
    total = None
    for k, tap in taps:
        if k == 0:
            part = mid
        elif k > 0:
            s = k * step
            part = pltpu.roll(jnp.where(at < s, high, mid), width - s, mid.ndim - 1)
        else:
            s = -k * step
            part = pltpu.roll(jnp.where(at >= width - s, low, mid), s, mid.ndim - 1)
        part = part * tap
        total = part if total is None else total + part
    return total


PARTNERS = [(dx, 0, dz) for dx in (-1, 0, 1) for dz in (-1, 0, 1) if dx or dz] + [(0, 1, 0), (0, -1, 0)]
UNROLL = {"stage": 16, "z": 2, "source": 4, "corr": 4, "sub": 4, "x": 1}
ZW = 4


def loop(name, n, body, init):
    width = min(UNROLL[name], n)
    if n % width:
        width = 1
    if width == n:
        for i in range(n):
            init = body(i, init)
        return init

    def step(j, carry):
        for k in range(width):
            carry = body(j * width + k, carry)
        return carry

    return lax.fori_loop(0, n // width, step, init)


def turn(value, shift):
    return value if isinstance(shift, int) and shift == 0 else pltpu.roll(value, shift, 1)


def modulo(a, n):
    return a % n if isinstance(a, int) else lax.rem(a, n)


def kernel(sizes, w_hbm, wave_hbm, ext_hbm, out_ref, corr_ref, scale_ref,
           wb, sb, yb, psi, va, pack, zin, ypack, yin, bands, ext_ref, w_ref, sums, sums2,
           send, recv, send2, recv2, local):
    nx, ny, nz = sizes
    cx, cy, cz = wave_hbm.shape
    wave_ref = wb.at[pl.ds(R, cx), pl.ds(R, cy)]
    get_wave = pltpu.make_async_copy(wave_hbm, wave_ref, local.at[0])
    get_ext = pltpu.make_async_copy(ext_hbm, ext_ref, local.at[1])
    get_weights = pltpu.make_async_copy(w_hbm, w_ref, local.at[2])
    get_wave.start()
    get_weights.start()
    ix, iy, iz = (lax.axis_index(a) for a in AXES)
    plane = nx * nz
    per = cz // cx
    here = ix * nz + iz

    def plane_id(d):
        t = lax.rem(here + d, plane)
        return t, {"gx": lax.div(t, nz), "gz": lax.rem(t, nz)}

    def line_id(d):
        t = lax.rem(iy + d, ny)
        return t, {"gy": t}

    barrier = pltpu.get_barrier_semaphore()

    def greet(ids):
        def body(d, c):
            pl.semaphore_signal(barrier, inc=1, device_id=ids(d)[1], device_id_type=MESH)
            return c
        return body

    near = nx <= 4 and ny <= 4 and nz <= 2
    if near:
        guests = 0
        for dx, dy, dz in PARTNERS:
            there = None
            target = {}
            for name, d, i, n in zip(AXES, (dx, dy, dz), (ix, iy, iz), sizes):
                if d:
                    ok = i < n - 1 if d > 0 else i > 0
                    there = ok if there is None else there & ok
                    target[name] = jnp.clip(i + d, 0, n - 1)
            guests += there.astype(jnp.int32)

            @pl.when(there)
            def _(target=target):
                pl.semaphore_signal(barrier, inc=1, device_id=target, device_id_type=MESH)
    else:
        guests = plane - 1 + ny - 1
        lax.fori_loop(1, plane, greet(plane_id), 0)
        lax.fori_loop(1, ny, greet(line_id), 0)

    counter = [0]

    def message(src, dst, dx, dy, dz):
        k = counter[0]
        counter[0] += 1
        to, back = None, None
        for d, i, n in ((dx, ix, nx), (dy, iy, ny), (dz, iz, nz)):
            if d > 0:
                a, b = i < n - 1, i > 0
            elif d < 0:
                a, b = i > 0, i < n - 1
            else:
                continue
            to = a if to is None else to & a
            back = b if back is None else back & b
        target = {}
        for name, d, i, n in zip(AXES, (dx, dy, dz), (ix, iy, iz), sizes):
            if d:
                target[name] = jnp.clip(i + d, 0, n - 1)
        copy = pltpu.make_async_remote_copy(
            src_ref=src, dst_ref=dst, send_sem=send.at[k], recv_sem=recv.at[k],
            device_id=target, device_id_type=MESH)
        return copy, to, back, dst

    sent = []

    def start(messages):
        for copy, to, _, _ in messages:
            pl.when(to)(copy.start)
            sent.append((copy, to))

    def blank(messages):
        for _, _, back, dst in messages:
            @pl.when(jnp.logical_not(back))
            def _(dst=dst):
                dst[...] = jnp.zeros(dst.shape, dst.dtype)

    def arrive(messages):
        for copy, _, back, _ in messages:
            pl.when(back)(copy.wait_recv)

    at = lanes((cy, cz))
    zero = jnp.zeros((cy, cz), jnp.float32)

    def pack_one(i, value, packs):
        mine = (at >= per * i) & (at < per * i + per)
        low = turn(value, per * i)
        high = turn(value, modulo(per * i + per, cz))
        return jnp.where(mine, low, packs[0]), jnp.where(mine, high, packs[1])

    def unpack(i, from_low, from_high):
        a = turn(from_high, modulo(cz - per * i, cz))
        b = turn(from_low, cz - per - per * i)
        return jnp.where(lanes(a.shape) < per, a, b)

    def pack_out(slot, packs):
        pack[slot, 0] = packs[0]
        pack[slot, 1] = packs[1]

    def z_messages(slot, across):
        out = []
        for dx in ((-1, 0, 1) if across else (0,)):
            out.append(message(pack.at[slot, 1], zin.at[slot, 0, 1 - dx], dx, 0, 1))
            out.append(message(pack.at[slot, 0], zin.at[slot, 1, 1 - dx], dx, 0, -1))
        return out

    def stage(i, packs):
        return pack_one(i, wave_ref[i], packs)

    get_wave.wait()

    pack_out(0, loop("stage", cx, stage, (zero, zero)))

    outer = [(0, R), (cy - R, R)]
    inner = [(R, cy - 2 * R)] if cy > 2 * R else []

    def x_messages(buf, y_at, bands_of_rows):
        out = []
        for first, rows in bands_of_rows:
            rows = pl.ds(y_at + first, rows)
            out.append(message(buf.at[pl.ds(cx, R), rows], buf.at[pl.ds(0, R), rows], 1, 0, 0))
            out.append(message(buf.at[pl.ds(R, R), rows], buf.at[pl.ds(R + cx, R), rows], -1, 0, 0))
        return out

    wave_x, wave_in = x_messages(wb, R, outer), x_messages(wb, R, inner)
    wave_z = z_messages(0, True)
    wave_y = [
        message(wave_ref.at[:, pl.ds(cy - R, R)], wb.at[pl.ds(R, cx), pl.ds(0, R)], 0, 1, 0),
        message(wave_ref.at[:, pl.ds(0, R)], wb.at[pl.ds(R, cx), pl.ds(R + cy, R)], 0, -1, 0),
    ]

    def y_messages(buf):
        return [
            message(buf.at[:, pl.ds(cy, R)], buf.at[:, pl.ds(0, R)], 0, 1, 0),
            message(buf.at[:, pl.ds(R, R)], buf.at[:, pl.ds(R + cy, R)], 0, -1, 0),
        ]

    mid_y = y_messages(yb.at[0])
    src_x, src_in = x_messages(sb, 0, outer), x_messages(sb, 0, inner)
    src_z = z_messages(1, True)
    end_y = y_messages(yb.at[1])

    psi_moves = []
    for s in range(SUBSTEPS - 1):
        buf = psi.at[s]
        moves = [
            message(buf.at[pl.ds(cx, H), pl.ds(R, cy)], buf.at[pl.ds(0, H), pl.ds(R, cy)], 1, 0, 0),
            message(buf.at[pl.ds(H, H), pl.ds(R, cy)], buf.at[pl.ds(H + cx, H), pl.ds(R, cy)], -1, 0, 0),
        ]
        moves += [
            message(ypack.at[s, 1], yin.at[s, 0], 0, 1, 0),
            message(ypack.at[s, 0], yin.at[s, 1], 0, -1, 0),
        ]
        moves += z_messages(2 + s, False)
        psi_moves.append(moves)

    pl.semaphore_wait(barrier, guests)
    start(wave_x + wave_z + wave_in + wave_y)
    get_ext.start()
    get_weights.wait()
    for group in [wave_x, wave_in, wave_z, wave_y, mid_y, src_x, src_in, src_z, end_y] + psi_moves:
        blank(group)

    def taps_of(dim, flip):
        return [(k, w_ref[dim, R - k if flip else R + k]) for k in range(-R, R + 1)]

    row = lax.broadcasted_iota(jnp.int32, (cz, cz), 0)
    gap = row - lanes((cz, cz))

    def band(slot, taps):
        inner = jnp.zeros((cz, cz), jnp.float32)
        outer = inner
        for k, tap in taps:
            inner = jnp.where(gap == k, tap, inner)
            if k:
                outer = jnp.where(gap == (k - cz if k > 0 else k + cz), tap, outer)
        bands[slot, pl.ds(0, cz)] = inner
        bands[slot, pl.ds(cz, cz)] = outer

    def along_z(values, nears, slot):
        both = jnp.concatenate([jnp.concatenate(values, 0), jnp.concatenate(nears, 0)], 1)
        return jnp.dot(both, bands[slot], precision=lax.Precision.HIGHEST,
                       preferred_element_type=jnp.float32)

    band(0, taps_of(2, False))
    band(1, taps_of(2, True))

    def smear_xz(src, y_at, slot, square, flip, buf, late, leave):
        taps = taps_of(0, flip)
        sides = []
        for side in range(2):
            near = [zin[slot, side, place] for place in range(3)]
            if square:
                near = [v * v for v in near]
            sides.append(lane_taps(near[1], near[0], near[2], per, taps))

        def tile(first):
            ins = [src[k, pl.ds(y_at + first, 8)] for k in range(cx + 2 * R)]
            if square:
                ins = [v * v for v in ins]
            outs = []
            for i in range(cx):
                total = None
                for k, tap in taps:
                    part = ins[i + R + k] * tap
                    total = part if total is None else total + part
                outs.append(total)
            below, above = (v[first:first + 8] for v in sides)
            made = along_z(outs, [unpack(i, below, above) for i in range(cx)], int(flip))
            for i in range(cx):
                buf[i, pl.ds(R + first, 8)] = made[8 * i:8 * i + 8]

        for first, rows in outer:
            for f in range(first, first + rows, 8):
                tile(f)
        start(leave)
        arrive(late)
        for first, rows in inner:
            for f in range(first, first + rows, 8):
                tile(f)
        arrive(leave)

    def smear_y(buf, i, taps):
        total = None
        for k, tap in taps:
            part = buf[i, pl.ds(R + k, cy)] * tap
            total = part if total is None else total + part
        return total

    arrive(wave_x + wave_z)
    smear_xz(wb, R, 0, True, False, yb.at[0], wave_in, mid_y)
    taps_y = taps_of(1, False)

    def source_pass(i, packs):
        coarse = smear_y(yb.at[0], i, taps_y)
        value = wave_ref[i]
        dens = value * value
        both = coarse * coarse
        source = 0.5 * dens * both - dens * coarse
        corr_ref[i] = (0.5 / 3.0) * both * coarse - 0.5 * both
        sb[R + i] = source
        return pack_one(i, source, packs)

    pack_out(1, loop("source", cx, source_pass, (zero, zero)))

    start(src_x + src_z + src_in)
    arrive(src_x + src_z)
    smear_xz(sb, 0, 1, False, True, yb.at[1], src_in, end_y)
    taps_yt = taps_of(1, True)

    get_ext.wait()

    def corr_pass(i, c):
        corr = corr_ref[i] + smear_y(yb.at[1], i, taps_yt)
        corr_ref[i] = corr
        va[i] = (1.0 + STEP * 0.5 * 3.0 * LAP_COEF[0]) - STEP * (corr + ext_ref[i])
        return c

    loop("corr", cx, corr_pass, 0)

    gains = [STEP * 0.5 * c for c in LAP_COEF]

    band(2, [(k, gains[abs(k)]) for k in range(-H, H + 1) if k])

    def advance(buf, reach, these, below, above):
        centers = [buf[reach + i, pl.ds(R, cy)] for i in these]
        along = along_z(centers, [unpack(i, below, above) for i in these], 2)
        made = []
        for at_, i in enumerate(these):
            total = centers[at_] * va[i] + along[at_ * cy:(at_ + 1) * cy]
            for k in range(1, H + 1):
                pair = buf[reach + i + k, pl.ds(R, cy)] + buf[reach + i - k, pl.ds(R, cy)]
                pair += buf[reach + i, pl.ds(R + k, cy)] + buf[reach + i, pl.ds(R - k, cy)]
                total += gains[k] * pair
            made.append(total)
        return made

    groups = [list(range(g, g + ZW)) for g in range(0, cx, ZW)]
    groups = groups[:1] + groups[-1:] + groups[1:-1]
    arrive(wave_y)
    buf, reach, slot = wb, R, 0
    for s in range(SUBSTEPS):
        if s:
            arrive(psi_moves[s - 1])
            for i in range(cx):
                half = pl.ds(H * (i % 2), H)
                buf[H + i, pl.ds(R - H, H)] = yin[s - 1, 0, i // 2, half]
                buf[H + i, pl.ds(R + cy, H)] = yin[s - 1, 1, i // 2, half]
        below, above = zin[slot, 0, 1], zin[slot, 1, 1]
        if s < SUBSTEPS - 1:
            after = psi.at[s]
            packs = (zero, zero)
            for n_, these in enumerate(groups):
                for i, value in zip(these, advance(buf, reach, these, below, above)):
                    after[H + i, pl.ds(R, cy)] = value
                    packs = pack_one(i, value, packs)
                    half = pl.ds(H * (i % 2), H)
                    ypack[s, 0, i // 2, half] = value[:H]
                    ypack[s, 1, i // 2, half] = value[cy - H:]
                if n_ == 1:
                    start(psi_moves[s][:2])
            pack_out(2 + s, packs)
            start(psi_moves[s][2:])
            buf, reach, slot = after, H, 2 + s
        else:
            total = zero
            for these in groups:
                for i, value in zip(these, advance(buf, reach, these, below, above)):
                    out_ref[i] = value
                    total = total + value * value

    part = jnp.sum(total, axis=0, keepdims=True)
    everyone = plane * ny
    me = iy * plane + here

    def any_id(d):
        t = lax.rem(me + d, everyone)
        p = lax.rem(t, plane)
        return t, {"gx": lax.div(p, nz), "gy": lax.div(t, plane), "gz": lax.rem(p, nz)}

    def all_sum(part, slots, ssem, rsem, me, n, ids):
        if n == 1:
            return part
        slots[me] = part

        def copy_of(d, slot):
            return pltpu.make_async_remote_copy(
                src_ref=slots.at[me], dst_ref=slots.at[slot], send_sem=ssem.at[d], recv_sem=rsem.at[slot],
                device_id=ids(d)[1], device_id_type=MESH)

        def go(d, c):
            copy_of(d, me).start()
            return c

        def come(d, c):
            copy_of(d, ids(d)[0]).wait_recv()
            return c

        def left(d, c):
            copy_of(d, me).wait_send()
            return c

        lax.fori_loop(1, n, go, 0)
        lax.fori_loop(1, n, come, 0)
        total = jnp.sum(slots[...], axis=0)
        lax.fori_loop(1, n, left, 0)
        return total

    if near:
        part = all_sum(part, sums, send2.at[0], recv2.at[0], me, everyone, any_id)
    else:
        part = all_sum(part, sums, send2.at[0], recv2.at[0], here, plane, plane_id)
        part = all_sum(part, sums2, send2.at[1], recv2.at[1], iy, ny, line_id)
    cells = float(cx * cy * cz * nx * ny * nz)
    scale_ref[...] = lax.rsqrt(jnp.full(scale_ref.shape, jnp.sum(part), jnp.float32) / cells + 1e-06)
    for copy, to in sent:
        pl.when(to)(copy.wait_send)


def shards(sizes, wave, external, weights):
    cx, cy, cz = wave.shape
    nx, ny, nz = sizes
    f32 = jnp.float32
    n_messages = 44
    summed = nx * ny * nz if nx <= 4 and ny <= 4 and nz <= 2 else nx * nz
    most = max(summed, ny)
    vmem = pl.BlockSpec(memory_space=pltpu.VMEM)
    stay = pl.BlockSpec(memory_space=pltpu.HBM)
    psi, corr, scale = pl.pallas_call(
        functools.partial(kernel, sizes),
        out_shape=(jax.ShapeDtypeStruct(wave.shape, f32), jax.ShapeDtypeStruct(wave.shape, f32),
                   jax.ShapeDtypeStruct((8, cz), f32)),
        in_specs=[stay, stay, stay],
        out_specs=(vmem, vmem, vmem),
        scratch_shapes=[
            pltpu.VMEM((cx + 2 * R, cy + 2 * R, cz), f32),
            pltpu.VMEM((cx + 2 * R, cy, cz), f32),
            pltpu.VMEM((2, cx, cy + 2 * R, cz), f32),
            pltpu.VMEM((SUBSTEPS - 1, cx + 2 * H, cy + 2 * R, cz), f32),
            pltpu.VMEM((cx, cy, cz), f32),
            pltpu.VMEM((SUBSTEPS + 1, 2, cy, cz), f32),
            pltpu.VMEM((SUBSTEPS + 1, 2, 3, cy, cz), f32),
            pltpu.VMEM((SUBSTEPS - 1, 2, cx // 2, 2 * H, cz), f32),
            pltpu.VMEM((SUBSTEPS - 1, 2, cx // 2, 2 * H, cz), f32),
            pltpu.VMEM((3, 2 * cz, cz), f32),
            pltpu.VMEM((cx, cy, cz), f32),
            pltpu.SMEM(weights.shape, f32),
            pltpu.VMEM((summed, 1, cz), f32),
            pltpu.VMEM((ny, 1, cz), f32),
            pltpu.SemaphoreType.DMA((n_messages,)),
            pltpu.SemaphoreType.DMA((n_messages,)),
            pltpu.SemaphoreType.DMA((2, most)),
            pltpu.SemaphoreType.DMA((2, most)),
            pltpu.SemaphoreType.DMA((3,)),
        ],
        compiler_params=pltpu.CompilerParams(collective_id=0, has_side_effects=True,
                                             vmem_limit_bytes=48 * 1024 * 1024),
    )(*[pltpu.with_memory_space_constraint(x, pltpu.HBM) for x in (weights, wave, external)])
    return psi * scale[0, 0], corr


def solution(mesh):
    sizes = tuple(mesh.shape[a] for a in AXES)
    spec = P(*AXES)
    return jax.shard_map(
        functools.partial(shards, sizes),
        mesh=mesh,
        in_specs=(spec, spec, P()),
        out_specs=(spec, spec),
        check_vma=False,
    )
```

```python
import functools

import jax
import jax.numpy as jnp
from jax import lax
from jax.experimental import pallas as pl
from jax.experimental.pallas import tpu as pltpu
from jax.sharding import PartitionSpec as P

SUBSTEPS = 3
LAP_COEF = (-205.0 / 72.0, 8.0 / 5.0, -1.0 / 5.0, 8.0 / 315.0, -1.0 / 560.0)
STEP = 0.08
AXES = ("gx", "gy", "gz")
MESH = pl.DeviceIdType.MESH
R = 8
H = 4


def lanes(shape):
    return lax.broadcasted_iota(jnp.int32, shape, len(shape) - 1)


def lane_taps(mid, low, high, step, taps):
    at = lanes(mid.shape)
    width = mid.shape[-1]
    total = None
    for k, tap in taps:
        if k == 0:
            part = mid
        elif k > 0:
            s = k * step
            part = pltpu.roll(jnp.where(at < s, high, mid), width - s, mid.ndim - 1)
        else:
            s = -k * step
            part = pltpu.roll(jnp.where(at >= width - s, low, mid), s, mid.ndim - 1)
        part = part * tap
        total = part if total is None else total + part
    return total


PARTNERS = [(dx, 0, dz) for dx in (-1, 0, 1) for dz in (-1, 0, 1) if dx or dz] + [(0, 1, 0), (0, -1, 0)]
UNROLL = {"stage": 16, "source": 16, "corr": 16}
ZW = 4


def loop(name, n, body, init):
    width = min(UNROLL[name], n)
    if n % width:
        width = 1
    if width == n:
        for i in range(n):
            init = body(i, init)
        return init

    def step(j, carry):
        for k in range(width):
            carry = body(j * width + k, carry)
        return carry

    return lax.fori_loop(0, n // width, step, init)


def turn(value, shift):
    return value if isinstance(shift, int) and shift == 0 else pltpu.roll(value, shift, 1)


def modulo(a, n):
    return a % n if isinstance(a, int) else lax.rem(a, n)


def kernel(sizes, w_hbm, wave_hbm, ext_hbm, out_ref, corr_ref, scale_ref,
           wb, sb, yb, psi, va, pack, zin, ypack, yin, bands, ext_ref, w_ref, sums, sums2,
           send, recv, send2, recv2, local):
    nx, ny, nz = sizes
    cx, cy, cz = wave_hbm.shape
    wave_ref = wb.at[pl.ds(R, cx), pl.ds(R, cy)]
    get_wave = pltpu.make_async_copy(wave_hbm, wave_ref, local.at[0])
    get_ext = pltpu.make_async_copy(ext_hbm, ext_ref, local.at[1])
    get_weights = pltpu.make_async_copy(w_hbm, w_ref, local.at[2])
    get_wave.start()
    get_weights.start()
    ix, iy, iz = (lax.axis_index(a) for a in AXES)
    plane = nx * nz
    per = cz // cx
    here = ix * nz + iz

    def plane_id(d):
        t = lax.rem(here + d, plane)
        return t, {"gx": lax.div(t, nz), "gz": lax.rem(t, nz)}

    def line_id(d):
        t = lax.rem(iy + d, ny)
        return t, {"gy": t}

    barrier = pltpu.get_barrier_semaphore()

    def greet(ids):
        def body(d, c):
            pl.semaphore_signal(barrier, inc=1, device_id=ids(d)[1], device_id_type=MESH)
            return c
        return body

    near = nx <= 4 and ny <= 4 and nz <= 2
    if near:
        guests = 0
        for dx, dy, dz in PARTNERS:
            there = None
            target = {}
            for name, d, i, n in zip(AXES, (dx, dy, dz), (ix, iy, iz), sizes):
                if d:
                    ok = i < n - 1 if d > 0 else i > 0
                    there = ok if there is None else there & ok
                    target[name] = jnp.clip(i + d, 0, n - 1)
            guests += there.astype(jnp.int32)

            @pl.when(there)
            def _(target=target):
                pl.semaphore_signal(barrier, inc=1, device_id=target, device_id_type=MESH)
    else:
        guests = plane - 1 + ny - 1
        lax.fori_loop(1, plane, greet(plane_id), 0)
        lax.fori_loop(1, ny, greet(line_id), 0)

    counter = [0]

    def message(src, dst, dx, dy, dz):
        k = counter[0]
        counter[0] += 1
        to, back = None, None
        for d, i, n in ((dx, ix, nx), (dy, iy, ny), (dz, iz, nz)):
            if d > 0:
                a, b = i < n - 1, i > 0
            elif d < 0:
                a, b = i > 0, i < n - 1
            else:
                continue
            to = a if to is None else to & a
            back = b if back is None else back & b
        target = {}
        for name, d, i, n in zip(AXES, (dx, dy, dz), (ix, iy, iz), sizes):
            if d:
                target[name] = jnp.clip(i + d, 0, n - 1)
        copy = pltpu.make_async_remote_copy(
            src_ref=src, dst_ref=dst, send_sem=send.at[k], recv_sem=recv.at[k],
            device_id=target, device_id_type=MESH)
        return copy, to, back, dst

    sent = []

    def start(messages):
        for copy, to, _, _ in messages:
            pl.when(to)(copy.start)
            sent.append((copy, to))

    def blank(messages):
        for _, _, back, dst in messages:
            @pl.when(jnp.logical_not(back))
            def _(dst=dst):
                dst[...] = jnp.zeros(dst.shape, dst.dtype)

    def arrive(messages):
        for copy, _, back, _ in messages:
            pl.when(back)(copy.wait_recv)

    at = lanes((cy, cz))
    zero = jnp.zeros((cy, cz), jnp.float32)

    def pack_one(i, value, packs):
        mine = (at >= per * i) & (at < per * i + per)
        low = turn(value, per * i)
        high = turn(value, modulo(per * i + per, cz))
        return jnp.where(mine, low, packs[0]), jnp.where(mine, high, packs[1])

    def unpack(i, from_low, from_high):
        a = turn(from_high, modulo(cz - per * i, cz))
        b = turn(from_low, cz - per - per * i)
        return jnp.where(lanes(a.shape) < per, a, b)

    def pack_out(slot, packs):
        pack[slot, 0] = packs[0]
        pack[slot, 1] = packs[1]

    def z_messages(slot, across):
        out = []
        for dx in ((-1, 0, 1) if across else (0,)):
            out.append(message(pack.at[slot, 1], zin.at[slot, 0, 1 - dx], dx, 0, 1))
            out.append(message(pack.at[slot, 0], zin.at[slot, 1, 1 - dx], dx, 0, -1))
        return out

    def stage(i, packs):
        return pack_one(i, wave_ref[i], packs)

    get_wave.wait()

    pack_out(0, loop("stage", cx, stage, (zero, zero)))

    outer = [(0, R), (cy - R, R)]
    inner = [(R, cy - 2 * R)] if cy > 2 * R else []

    def x_messages(buf, y_at, bands_of_rows):
        out = []
        for first, rows in bands_of_rows:
            rows = pl.ds(y_at + first, rows)
            out.append(message(buf.at[pl.ds(cx, R), rows], buf.at[pl.ds(0, R), rows], 1, 0, 0))
            out.append(message(buf.at[pl.ds(R, R), rows], buf.at[pl.ds(R + cx, R), rows], -1, 0, 0))
        return out

    wave_x, wave_in = x_messages(wb, R, outer), x_messages(wb, R, inner)
    wave_z = z_messages(0, True)
    wave_y = [
        message(wave_ref.at[:, pl.ds(cy - R, R)], wb.at[pl.ds(R, cx), pl.ds(0, R)], 0, 1, 0),
        message(wave_ref.at[:, pl.ds(0, R)], wb.at[pl.ds(R, cx), pl.ds(R + cy, R)], 0, -1, 0),
    ]

    def y_messages(buf):
        return [
            message(buf.at[:, pl.ds(cy, R)], buf.at[:, pl.ds(0, R)], 0, 1, 0),
            message(buf.at[:, pl.ds(R, R)], buf.at[:, pl.ds(R + cy, R)], 0, -1, 0),
        ]

    mid_y = y_messages(yb.at[0])
    src_x, src_in = x_messages(sb, 0, outer), x_messages(sb, 0, inner)
    src_z = z_messages(1, True)
    end_y = y_messages(yb.at[1])

    psi_moves = []
    for s in range(SUBSTEPS - 1):
        buf = psi.at[s]
        moves = [
            message(buf.at[pl.ds(cx, H), pl.ds(R, cy)], buf.at[pl.ds(0, H), pl.ds(R, cy)], 1, 0, 0),
            message(buf.at[pl.ds(H, H), pl.ds(R, cy)], buf.at[pl.ds(H + cx, H), pl.ds(R, cy)], -1, 0, 0),
        ]
        moves += [
            message(ypack.at[s, 1], yin.at[s, 0], 0, 1, 0),
            message(ypack.at[s, 0], yin.at[s, 1], 0, -1, 0),
        ]
        moves += z_messages(2 + s, False)
        psi_moves.append(moves)

    pl.semaphore_wait(barrier, guests)
    start(wave_x + wave_z + wave_in + wave_y)
    get_ext.start()
    get_weights.wait()
    for group in [wave_x, wave_in, wave_z, wave_y, mid_y, src_x, src_in, src_z, end_y] + psi_moves:
        blank(group)

    def taps_of(dim, flip):
        return [(k, w_ref[dim, R - k if flip else R + k]) for k in range(-R, R + 1)]

    row = lax.broadcasted_iota(jnp.int32, (cz, cz), 0)
    gap = row - lanes((cz, cz))

    def band(slot, taps):
        inner = jnp.zeros((cz, cz), jnp.float32)
        outer = inner
        for k, tap in taps:
            inner = jnp.where(gap == k, tap, inner)
            if k:
                outer = jnp.where(gap == (k - cz if k > 0 else k + cz), tap, outer)
        bands[slot, pl.ds(0, cz)] = inner
        bands[slot, pl.ds(cz, cz)] = outer

    def along_z(values, nears, slot):
        both = jnp.concatenate([jnp.concatenate(values, 0), jnp.concatenate(nears, 0)], 1)
        return jnp.dot(both, bands[slot], precision=lax.Precision.HIGHEST,
                       preferred_element_type=jnp.float32)

    band(0, taps_of(2, False))
    band(1, taps_of(2, True))
    gains = [STEP * 0.5 * c for c in LAP_COEF]
    band(2, [(k, gains[abs(k)]) for k in range(-H, H + 1) if k])

    def smear_xz(src, y_at, slot, square, flip, buf, late, leave):
        taps = taps_of(0, flip)
        sides = []
        for side in range(2):
            near = [zin[slot, side, place] for place in range(3)]
            if square:
                near = [v * v for v in near]
            sides.append(lane_taps(near[1], near[0], near[2], per, taps))

        def tile(first):
            ins = [src[k, pl.ds(y_at + first, 8)] for k in range(cx + 2 * R)]
            if square:
                ins = [v * v for v in ins]
            outs = []
            for i in range(cx):
                total = None
                for k, tap in taps:
                    part = ins[i + R + k] * tap
                    total = part if total is None else total + part
                outs.append(total)
            below, above = (v[first:first + 8] for v in sides)
            made = along_z(outs, [unpack(i, below, above) for i in range(cx)], int(flip))
            for i in range(cx):
                buf[i, pl.ds(R + first, 8)] = made[8 * i:8 * i + 8]

        for first, rows in outer:
            for f in range(first, first + rows, 8):
                tile(f)
        start(leave)
        arrive(late)
        for first, rows in inner:
            for f in range(first, first + rows, 8):
                tile(f)
        arrive(leave)

    def smear_y(buf, i, taps):
        total = None
        for k, tap in taps:
            part = buf[i, pl.ds(R + k, cy)] * tap
            total = part if total is None else total + part
        return total

    arrive(wave_x + wave_z)
    smear_xz(wb, R, 0, True, False, yb.at[0], wave_in, mid_y)
    taps_y = taps_of(1, False)

    def source_pass(i, packs):
        coarse = smear_y(yb.at[0], i, taps_y)
        value = wave_ref[i]
        dens = value * value
        both = coarse * coarse
        source = 0.5 * dens * both - dens * coarse
        corr_ref[i] = (0.5 / 3.0) * both * coarse - 0.5 * both
        sb[R + i] = source
        return pack_one(i, source, packs)

    pack_out(1, loop("source", cx, source_pass, (zero, zero)))

    start(src_x + src_z + src_in)
    arrive(src_x + src_z)
    smear_xz(sb, 0, 1, False, True, yb.at[1], src_in, end_y)
    taps_yt = taps_of(1, True)

    get_ext.wait()

    def corr_pass(i, c):
        corr = corr_ref[i] + smear_y(yb.at[1], i, taps_yt)
        corr_ref[i] = corr
        va[i] = (1.0 + STEP * 0.5 * 3.0 * LAP_COEF[0]) - STEP * (corr + ext_ref[i])
        return c

    loop("corr", cx, corr_pass, 0)


    def advance(buf, reach, these, below, above):
        centers = [buf[reach + i, pl.ds(R, cy)] for i in these]
        along = along_z(centers, [unpack(i, below, above) for i in these], 2)
        made = []
        for at_, i in enumerate(these):
            total = centers[at_] * va[i] + along[at_ * cy:(at_ + 1) * cy]
            for k in range(1, H + 1):
                pair = buf[reach + i + k, pl.ds(R, cy)] + buf[reach + i - k, pl.ds(R, cy)]
                pair += buf[reach + i, pl.ds(R + k, cy)] + buf[reach + i, pl.ds(R - k, cy)]
                total += gains[k] * pair
            made.append(total)
        return made

    groups = [list(range(g, g + ZW)) for g in range(0, cx, ZW)]
    groups = groups[:1] + groups[-1:] + groups[1:-1]
    arrive(wave_y)
    buf, reach, slot = wb, R, 0
    for s in range(SUBSTEPS):
        if s:
            arrive(psi_moves[s - 1])
            for i in range(cx):
                half = pl.ds(H * (i % 2), H)
                buf[H + i, pl.ds(R - H, H)] = yin[s - 1, 0, i // 2, half]
                buf[H + i, pl.ds(R + cy, H)] = yin[s - 1, 1, i // 2, half]
        below, above = zin[slot, 0, 1], zin[slot, 1, 1]
        if s < SUBSTEPS - 1:
            after = psi.at[s]
            packs = (zero, zero)
            for n_, these in enumerate(groups):
                for i, value in zip(these, advance(buf, reach, these, below, above)):
                    after[H + i, pl.ds(R, cy)] = value
                    packs = pack_one(i, value, packs)
                    half = pl.ds(H * (i % 2), H)
                    ypack[s, 0, i // 2, half] = value[:H]
                    ypack[s, 1, i // 2, half] = value[cy - H:]
                if n_ == 1:
                    start(psi_moves[s][:2])
            pack_out(2 + s, packs)
            start(psi_moves[s][2:])
            buf, reach, slot = after, H, 2 + s
        else:
            total = zero
            for these in groups:
                for i, value in zip(these, advance(buf, reach, these, below, above)):
                    out_ref[i] = value
                    total = total + value * value

    part = jnp.sum(total, axis=0, keepdims=True)
    everyone = plane * ny
    me = iy * plane + here

    def any_id(d):
        t = lax.rem(me + d, everyone)
        p = lax.rem(t, plane)
        return t, {"gx": lax.div(p, nz), "gy": lax.div(t, plane), "gz": lax.rem(p, nz)}

    def all_sum(part, slots, ssem, rsem, me, n, ids):
        if n == 1:
            return part
        slots[me] = part

        def copy_of(d, slot):
            return pltpu.make_async_remote_copy(
                src_ref=slots.at[me], dst_ref=slots.at[slot], send_sem=ssem.at[d], recv_sem=rsem.at[slot],
                device_id=ids(d)[1], device_id_type=MESH)

        def go(d, c):
            copy_of(d, me).start()
            return c

        def come(d, c):
            copy_of(d, ids(d)[0]).wait_recv()
            return c

        def left(d, c):
            copy_of(d, me).wait_send()
            return c

        lax.fori_loop(1, n, go, 0)
        lax.fori_loop(1, n, come, 0)
        total = jnp.sum(slots[...], axis=0)
        lax.fori_loop(1, n, left, 0)
        return total

    if near:
        part = all_sum(part, sums, send2.at[0], recv2.at[0], me, everyone, any_id)
    else:
        part = all_sum(part, sums, send2.at[0], recv2.at[0], here, plane, plane_id)
        part = all_sum(part, sums2, send2.at[1], recv2.at[1], iy, ny, line_id)
    cells = float(cx * cy * cz * nx * ny * nz)
    scale_ref[...] = lax.rsqrt(jnp.full(scale_ref.shape, jnp.sum(part), jnp.float32) / cells + 1e-06)
    for copy, to in sent:
        pl.when(to)(copy.wait_send)


def shards(sizes, wave, external, weights):
    cx, cy, cz = wave.shape
    nx, ny, nz = sizes
    f32 = jnp.float32
    n_messages = 44
    summed = nx * ny * nz if nx <= 4 and ny <= 4 and nz <= 2 else nx * nz
    most = max(summed, ny)
    vmem = pl.BlockSpec(memory_space=pltpu.VMEM)
    stay = pl.BlockSpec(memory_space=pltpu.HBM)
    psi, corr, scale = pl.pallas_call(
        functools.partial(kernel, sizes),
        out_shape=(jax.ShapeDtypeStruct(wave.shape, f32), jax.ShapeDtypeStruct(wave.shape, f32),
                   jax.ShapeDtypeStruct((8, cz), f32)),
        in_specs=[stay, stay, stay],
        out_specs=(vmem, vmem, vmem),
        scratch_shapes=[
            pltpu.VMEM((cx + 2 * R, cy + 2 * R, cz), f32),
            pltpu.VMEM((cx + 2 * R, cy, cz), f32),
            pltpu.VMEM((2, cx, cy + 2 * R, cz), f32),
            pltpu.VMEM((SUBSTEPS - 1, cx + 2 * H, cy + 2 * R, cz), f32),
            pltpu.VMEM((cx, cy, cz), f32),
            pltpu.VMEM((SUBSTEPS + 1, 2, cy, cz), f32),
            pltpu.VMEM((SUBSTEPS + 1, 2, 3, cy, cz), f32),
            pltpu.VMEM((SUBSTEPS - 1, 2, cx // 2, 2 * H, cz), f32),
            pltpu.VMEM((SUBSTEPS - 1, 2, cx // 2, 2 * H, cz), f32),
            pltpu.VMEM((3, 2 * cz, cz), f32),
            pltpu.VMEM((cx, cy, cz), f32),
            pltpu.SMEM(weights.shape, f32),
            pltpu.VMEM((summed, 1, cz), f32),
            pltpu.VMEM((ny, 1, cz), f32),
            pltpu.SemaphoreType.DMA((n_messages,)),
            pltpu.SemaphoreType.DMA((n_messages,)),
            pltpu.SemaphoreType.DMA((2, most)),
            pltpu.SemaphoreType.DMA((2, most)),
            pltpu.SemaphoreType.DMA((3,)),
        ],
        compiler_params=pltpu.CompilerParams(collective_id=0, has_side_effects=True,
                                             vmem_limit_bytes=48 * 1024 * 1024),
    )(*[pltpu.with_memory_space_constraint(x, pltpu.HBM) for x in (weights, wave, external)])
    return psi * scale[0, 0], corr


def solution(mesh):
    sizes = tuple(mesh.shape[a] for a in AXES)
    spec = P(*AXES)
    return jax.shard_map(
        functools.partial(shards, sizes),
        mesh=mesh,
        in_specs=(spec, spec, P()),
        out_specs=(spec, spec),
        check_vma=False,
    )
```
